512 devices in a mesh: rep: 2 (over core), ep: 64 (over z, y), dp: 4 (over x).
Axes of the slice: x: 4, y: 4, z: 16, core: 2. Of those that a mesh axis runs over, the one named last changes fastest.
Arguments:
- tokens: bfloat16 [16384, 2048], P(('rep', 'ep', 'dp')), may hold values from -6 to 6
- upstream: bfloat16 [16384, 2048], P(('rep', 'ep', 'dp')), may hold values from -6 to 6
- expert_ids: int32 [16384, 4], P(('rep', 'ep', 'dp')), may hold values from 0 to 63, all different within a row; in each aligned block of 32 rows (0 to 31, 32 to 63, ...) at most 4 rows name the same one
- route_weight: bfloat16 [16384, 4], P(('rep', 'ep', 'dp')), may hold values from 0.099609375 to 1
- gate_weight: bfloat16 [64, 384, 2048], P('ep', 'dp'), may hold values from -0.125 to 0.125
- up_weight: bfloat16 [64, 384, 2048], P('ep', 'dp'), may hold values from -0.125 to 0.125
- down_weight: bfloat16 [64, 384, 2048], P('ep', 'dp'), may hold values from -0.3125 to 0.3125
Outputs:
- d_tokens: bfloat16 [16384, 2048], P(('rep', 'ep', 'dp'))
- d_probs: bfloat16 [16384, 4], P(('rep', 'ep', 'dp'))
- grad_down: float32 [64, 384, 2048], P('ep', 'dp')
The draws below stay inside these ranges and needn't reach their ends.
Inputs may be any that keep to these rules, and one draw needn't show every extreme that they name: `expert_ids`: each row names 4 different experts; among the rows of one device no expert is named by more than 4 rows, and in every draw some expert is named by exactly 4 rows of some device.
All inputs are finite; a program needn't handle non-finite values.
Results may differ from the reference program's by a relative error of at most 0.012.
Values may be sent and summed in bfloat16 or wider, within the bound.
A program may use at most 64 MiB of HBM per device.

```python
import math
import jax
import jax.numpy as jnp
import numpy as np
from jax import lax

D = 2048
FF = 384
TOK_DEV = 32
EXPERTS = 64
TOP = 4
CAP = 4
TOKENS = 16384


def shard_levels(key, dims, cuts, smallest, high):
    level, own = 1.0, jax.random.fold_in(key, 6)
    for position, shards_of in cuts:
        heights = jnp.exp(jax.random.uniform(jax.random.fold_in(own, position), (shards_of,), jnp.float32, smallest / len(cuts), high / len(cuts)))
        level = level * jnp.repeat(heights, dims[position] // shards_of).reshape([-1 if axis == position else 1 for axis in range(len(dims))])
    return level


def deal_out(rng, own, number, rows, count, top, most, lean):
    sequence = jax.random.permutation(rng, count)
    crowded, usual = portions_of(count, rows * top, most, lean, True), portions_of(count, rows * top, most, lean, False)
    places = jnp.arange(count)

    def named(tallies, offset_by):
        used = int((tallies > 0).sum())
        fixed = max(1, used // 4)
        shifted = fixed + (places - fixed + offset_by * (used - fixed)) % max(1, count - fixed)
        return jnp.zeros((count,), jnp.int32).at[sequence[jnp.where(places < fixed, places, shifted)]].set(jnp.asarray(tallies, jnp.int32))

    tallies = jnp.where(number % 4 == 0, named(crowded, number // 4), named(usual, number - number // 4 - 1))
    mixed = jax.random.permutation(jax.random.fold_in(own, 3), count)
    donor, sink = mixed[0:count // 2 * 2:2], mixed[1:count // 2 * 2:2]
    room = jnp.minimum(tallies[donor] - 1, most - tallies[sink]) // 2
    room = jnp.where((donor == sequence[0]) | (sink == sequence[0]) | (tallies[sink] == 0), 0, jnp.maximum(room, 0))
    shifted = jax.random.randint(jax.random.fold_in(own, 4), (count // 2,), 0, 1 << 20) % (room + 1)
    tallies = tallies.at[donor].add(-shifted).at[sink].add(shifted)
    items = jnp.searchsorted(jnp.cumsum(tallies), jnp.arange(rows * top), side="right").astype(jnp.int32)
    table = items.reshape(top, rows).T
    table = table[jax.random.permutation(jax.random.fold_in(own, 1), rows)]
    offset_by = jax.random.randint(jax.random.fold_in(own, 2), (rows, 1), 0, top)
    return jnp.take_along_axis(table, (jnp.arange(top)[None, :] + offset_by) % top, axis=1)


def portions_of(count, total, limit, lean, full):
    loads = [(1 << 20) // math.isqrt(grade ** lean) + 1 for grade in range(1, count + 1)]
    largest = limit if full else min(limit, max(-(-total // count), total * loads[0] // sum(loads)))
    least = 1 if total - largest >= count - 1 else 0
    given, surplus = [largest] + [least] * (count - 1), total - largest - least * (count - 1)
    while surplus > 0:
        candidates = [i for i in range(1, count) if given[i] < largest] or [i for i in range(1, count) if given[i] < limit]
        whole, left = sum([loads[i] for i in candidates]), surplus
        for i in candidates:
            extra = min(limit - given[i], max(1, left * loads[i] // whole), surplus)
            given[i] = given[i] + extra
            surplus = surplus - extra
    return np.array(given)


def bell_draw(key, dims, scale, most, split=(), kind=jnp.bfloat16):
    loudness = shard_levels(key, dims, split, -0.22, 0.18) if split else 1.0
    drawn = jax.random.normal(key, dims, jnp.float32) * scale * loudness
    return jnp.minimum(jnp.maximum(drawn, -most), most).astype(kind)


def setup_inputs(seed: int = 0) -> dict:
    seeds = jax.random.split(jax.random.key(seed), 8)
    tokens = bell_draw(seeds[0], (TOKENS, D), 1.0, 6.0, ((0, 512),))
    upstream = bell_draw(seeds[1], (TOKENS, D), 1.0, 6.0, ((0, 512),))
    expert_ids_keys = jax.random.split(jax.random.fold_in(seeds[2], 1), TOKENS // TOK_DEV)
    expert_ids_turns = jax.random.permutation(jax.random.fold_in(seeds[2], 3), TOKENS // TOK_DEV)
    expert_ids = jax.vmap(lambda own, number: deal_out(jax.random.fold_in(seeds[2], 2), own, number, TOK_DEV, EXPERTS, TOP, CAP, 1))(expert_ids_keys, expert_ids_turns).reshape((TOKENS, TOP))
    route_weight = jnp.clip(0.099609375 + 0.9003906 * jax.random.uniform(seeds[3], (TOKENS, TOP), jnp.float32) ** shard_levels(seeds[3], (TOKENS, TOP), ((0, 512),), -0.2, 0.2), 0.099609375, 1.0).astype(jnp.bfloat16)
    gate_weight = bell_draw(seeds[4], (EXPERTS, FF, D), D ** -0.5, 0.125, ((0, 64), (1, 4)))
    up_weight = bell_draw(seeds[5], (EXPERTS, FF, D), D ** -0.5, 0.125, ((0, 64), (1, 4)))
    down_weight = bell_draw(seeds[6], (EXPERTS, FF, D), FF ** -0.5, 0.3125, ((0, 64), (1, 4)))
    return dict(tokens=tokens, upstream=upstream, expert_ids=expert_ids, route_weight=route_weight, gate_weight=gate_weight, up_weight=up_weight, down_weight=down_weight)


def reference(tokens, upstream, expert_ids, route_weight, gate_weight, up_weight, down_weight):
    route_count = TOKENS * TOP
    most_rows = (TOKENS // TOK_DEV) * CAP
    flat_ids = expert_ids.reshape(route_count).astype(jnp.int32)
    tok_padded = jnp.concatenate([tokens, jnp.zeros((1, D), tokens.dtype)], axis=0)
    up_padded = jnp.concatenate([upstream, jnp.zeros((1, D), upstream.dtype)], axis=0)
    prob_padded = jnp.concatenate([route_weight.reshape(route_count), jnp.zeros((1,), route_weight.dtype)], axis=0)

    def one_expert(running, expert):
        dx_total, dprob_total = running
        row_index = jnp.nonzero(flat_ids == expert, size=most_rows, fill_value=route_count)[0].astype(jnp.int32)
        token_index = (row_index // TOP).astype(jnp.int32)
        x_rows = tok_padded[token_index]
        dy_rows = up_padded[token_index]
        weights = prob_padded[row_index]
        gate_mat = gate_weight[expert]
        up_mat = up_weight[expert]
        down_mat = down_weight[expert]
        gate_pre = jnp.dot(x_rows, gate_mat.T, preferred_element_type=jnp.float32)
        up_pre = jnp.dot(x_rows, up_mat.T, preferred_element_type=jnp.float32)
        sig_gate = jax.nn.sigmoid(gate_pre)
        silu_gate = gate_pre * sig_gate
        act_rows = (silu_gate * up_pre).astype(jnp.bfloat16)
        expert_out = jnp.dot(act_rows, down_mat, preferred_element_type=jnp.float32)
        dprob_rows = jnp.sum(dy_rows.astype(jnp.float32) * expert_out, axis=-1).astype(jnp.bfloat16)
        d_out = (weights.astype(jnp.float32)[:, None] * dy_rows.astype(jnp.float32)).astype(jnp.bfloat16)
        d_act = jnp.dot(d_out, down_mat.T, preferred_element_type=jnp.float32)
        d_gate = (d_act * up_pre * sig_gate * (1.0 + gate_pre * (1.0 - sig_gate))).astype(jnp.bfloat16)
        d_up = (d_act * silu_gate).astype(jnp.bfloat16)
        route_dx = (jnp.dot(d_gate, gate_mat, preferred_element_type=jnp.float32)
                    + jnp.dot(d_up, up_mat, preferred_element_type=jnp.float32)).astype(jnp.bfloat16)
        grad_rows = jnp.dot(act_rows.T, d_out, preferred_element_type=jnp.float32)
        dx_total = dx_total.at[token_index].add(route_dx.astype(jnp.float32))
        dprob_total = dprob_total.at[row_index].set(dprob_rows.astype(jnp.float32))
        return (dx_total, dprob_total), grad_rows

    start_state = (jnp.zeros((TOKENS + 1, D), jnp.float32), jnp.zeros((route_count + 1,), jnp.float32))
    final_state, grad_down = lax.scan(one_expert, start_state, jnp.arange(EXPERTS, dtype=jnp.int32))
    dx_total, dprob_total = final_state
    d_tokens = dx_total[:TOKENS].astype(jnp.bfloat16)
    d_probs = dprob_total[:route_count].reshape(TOKENS, TOP).astype(jnp.bfloat16)
    return d_tokens, d_probs, grad_down
```

```python
import functools

import jax
import jax.numpy as jnp
from jax import lax
from jax.experimental import pallas as pl
from jax.experimental.pallas import tpu as pltpu
from jax.sharding import PartitionSpec as P

MESH = pl.DeviceIdType.MESH
F32, BF16 = jnp.float32, jnp.bfloat16
CAP = 4
LANES = 128
TILE = 512


def dot_t(left, right):
    return lax.dot_general(left, right, (((1,), (1,)), ((), ())), preferred_element_type=F32)


def dot_n(left, right):
    return lax.dot_general(left, right, (((1,), (0,)), ((), ())), preferred_element_type=F32)


def tiles(width):
    return [(start, min(TILE, width - start)) for start in range(0, width, TILE)]


def kernel(
    sizes, tok_ref, ups_ref, ids_ref, rw_ref, gate_ref, up_ref, down_ref,
    dtok_ref, dprob_ref, grad_ref,
    meta, xa, dya, seltr, stage, rows, weights, act, dxs, ret, part,
    fsend, frecv, bsend, brecv, gmine, gsend, gpart, ssend, srecv, gfin, gother,
    send_sem, recv_sem,
):
    nx, ny, nz = sizes
    tok, width = tok_ref.shape
    hid = gate_ref.shape[0]
    half_hid = hid // 2
    experts = ny * nz
    half = nz // 2
    batches = nz // 4
    wide = width + LANES
    mid = width // 2
    block = 4 * CAP
    core, ep, dp = lax.axis_index("rep"), lax.axis_index("ep"), lax.axis_index("dp")
    z, y = ep // ny, lax.rem(ep, ny)

    def at_z(step):
        return (core, lax.rem(z + step + nz, nz) * ny + y, dp)

    def at_y(step):
        return (core, z * ny + lax.rem(y + step, ny), dp)

    def at_x(step):
        return (core, ep, lax.rem(dp + step, nx))

    partner = (1 - core, ep, dp)

    order = [0]
    for step in range(1, half):
        order += [-step, step]
    order.append(half)
    place = {delta: index for index, delta in enumerate(order)}
    place[-half] = place[half]

    started = []

    def send(src, dst, device):
        index = len(started)
        copy = pltpu.make_async_remote_copy(
            src_ref=src, dst_ref=dst, send_sem=send_sem.at[index],
            recv_sem=recv_sem.at[index], device_id=device, device_id_type=MESH,
        )
        copy.start()
        started.append(copy)
        return copy

    barrier = pltpu.get_barrier_semaphore()
    peers = [at_z(1), at_z(-1), partner]
    peers += [at_y(step) for step in range(1, ny)]
    peers += [at_x(1)] if nx == 2 else [at_x(1), at_x(nx - 1)]
    if nx == 4:
        peers.append(at_x(2))
    for peer in peers:
        pl.semaphore_signal(barrier, inc=1, device_id=peer, device_id_type=MESH)
    pl.semaphore_wait(barrier, len(peers))

    xcopy, dcopy, mcopy = {}, {}, {}
    for sign in (-1, 1):
        there = xa.at[place[sign]]
        xcopy[sign] = send(tok_ref, there.at[:, pl.ds(0, width)], at_z(-sign))
    for sign in (-1, 1):
        dcopy[sign] = send(ups_ref, dya.at[place[sign]], at_z(-sign))

    lane = lax.broadcasted_iota(jnp.int32, (tok, LANES), 1)
    routed = jnp.zeros((tok, LANES), F32)
    scale = jnp.zeros((tok, LANES), F32)
    for k in range(4):
        name = ids_ref[:, k:k + 1]
        routed = routed + jnp.where(lane == name, 1.0, 0.0)
        scale = scale + jnp.where(lane == name + 64, rw_ref[:, k:k + 1].astype(F32), 0.0)
    lower = jnp.where(
        lax.broadcasted_iota(jnp.int32, (tok, tok), 1) < lax.broadcasted_iota(jnp.int32, (tok, tok), 0),
        1.0, 0.0,
    ).astype(BF16)
    rank = routed * (dot_n(lower, routed.astype(BF16)) + 1.0)
    own_meta = (rank + scale).astype(BF16)
    meta[...] = own_meta
    for sign in (-1, 1):
        there = xa.at[place[sign]]
        mcopy[sign] = send(meta, there.at[:, pl.ds(width, LANES)], at_z(-sign))

    shard_refs = (gate_ref, up_ref, down_ref)
    mine = pl.ds(pl.multiple_of(core * half_hid, half_hid), half_hid)
    theirs = pl.ds(pl.multiple_of((1 - core) * half_hid, half_hid), half_hid)
    wcopy = {}
    for index, ref in enumerate(shard_refs):
        wcopy[index, nx - 1] = send(ref.at[mine], weights.at[index, nx - 1, 0], at_x(1))
        if nx == 4:
            wcopy[index, 1] = send(ref.at[mine], weights.at[index, 1, 0], at_x(3))
    for index, ref in enumerate(shard_refs):
        weights[index, 0, 0] = ref[mine, :]
        weights[index, 0, 1] = ref[theirs, :]
    xa[0, :, 0:width] = tok_ref[...]
    xa[0, :, width:wide] = own_meta
    dya[0] = ups_ref[...]

    hcopy = []

    def near_weights():
        for index in range(3):
            wcopy[index, nx - 1].wait_recv()
            if nx == 4:
                wcopy[index, 1].wait_recv()
                if index == 1:
                    wcopy[index, 2] = send(weights.at[index, 1, 0], weights.at[index, 2, 0], at_x(3))
                else:
                    wcopy[index, 2] = send(weights.at[index, 3, 0], weights.at[index, 2, 0], at_x(1))
        for index in range(3):
            for rel in ((1, 3) if nx == 4 else (1,)):
                hcopy.append(send(weights.at[index, rel, 0], weights.at[index, rel, 1], partner))

    def far_weights():
        if nx == 4:
            for index in range(3):
                wcopy[index, 2].wait_recv()
                hcopy.append(send(weights.at[index, 2, 0], weights.at[index, 2, 1], partner))

    def all_weights():
        for copy in hcopy:
            copy.wait_recv()

    count = ny * block
    ycopy = {}

    def dispatch(b):
        group = xa[4 * b:4 * b + 4, :, width:wide].reshape(4 * tok, LANES)
        row = lax.broadcasted_iota(jnp.int32, (count, LANES), 0)
        col = lax.broadcasted_iota(jnp.int32, (count, LANES), 1)
        name = z * ny + lax.rem(y + row // block, ny)
        pick = jnp.where(col == name, 1.0, 0.0).astype(BF16)
        pick_w = jnp.where(col == name + 64, 1.0, 0.0).astype(BF16)

        def chosen(value, r, c):
            slot = (lax.rem(r, CAP) + 1).astype(F32)
            return (value == slot) & (c // tok == lax.rem(r // CAP, 4))

        shape = (count, 4 * tok)
        r, c = (lax.broadcasted_iota(jnp.int32, shape, axis) for axis in (0, 1))
        hit = chosen(dot_t(pick, group), r, c)
        sel = jnp.where(hit, 1.0, 0.0).astype(BF16)
        sel_w = jnp.where(hit, dot_t(pick_w, group), 0.0).astype(BF16)
        shape = (4 * tok, count)
        c, r = (lax.broadcasted_iota(jnp.int32, shape, axis) for axis in (0, 1))
        seltr[b] = jnp.where(chosen(dot_t(group, pick), r, c), 1.0, 0.0).astype(BF16)
        for start, size in tiles(width):
            for source, chooser, first in ((xa, sel, 0), (dya, sel_w, block)):
                value = source[4 * b:4 * b + 4, :, start:start + size].reshape(4 * tok, size)
                out = dot_n(chooser, value).astype(BF16).reshape(ny, block, size)
                rows[b, 0, first:first + block, start:start + size] = out[0]
                stage[b, 1:ny, first:first + block, start:start + size] = out[1:ny]
        for step in range(1, ny):
            ycopy[b, step] = send(stage.at[b, step], rows.at[b, ny - step], at_y(step))

    rcopy = {}

    def compute(b):
        for step in range(1, ny):
            ycopy[b, step].wait_recv()
        x_rows = rows[b, :, 0:block, :].reshape(count, width)
        d_rows = rows[b, :, block:2 * block, :].reshape(count, width)
        hidden = nx * hid
        gate_w = weights[0].reshape(hidden, width)
        up_w = weights[1].reshape(hidden, width)
        down_w = weights[2].reshape(hidden, width)
        gate_pre = dot_t(x_rows, gate_w)
        up_pre = dot_t(x_rows, up_w)
        d_act = dot_t(d_rows, down_w)
        sig = jax.nn.sigmoid(gate_pre)
        silu = gate_pre * sig
        act_rows = (silu * up_pre).astype(BF16)
        act[b] = act_rows
        d_gate = (d_act * up_pre * sig * (1.0 + gate_pre * (1.0 - sig))).astype(BF16)
        d_up = (d_act * silu).astype(BF16)
        prob = jnp.sum(act_rows.astype(F32) * d_act, axis=1, keepdims=True)
        here = lax.broadcasted_iota(jnp.int32, (count, LANES), 1) == ep
        extra = jnp.where(here, prob, 0.0).astype(BF16).reshape(ny, block, LANES)
        dxs[b, 1:ny, :, width:wide] = extra[1:ny]
        ret[b, 0, :, width:wide] = extra[0]
        for start, size in tiles(width):
            gate_t = weights[0, :, :, :, start:start + size].reshape(hidden, size)
            up_t = weights[1, :, :, :, start:start + size].reshape(hidden, size)
            out = (dot_n(d_gate, gate_t) + dot_n(d_up, up_t)).astype(BF16).reshape(ny, block, size)
            dxs[b, 1:ny, :, start:start + size] = out[1:ny]
            ret[b, 0, :, start:start + size] = out[0]
        for step in range(1, ny):
            rcopy[b, step] = send(dxs.at[b, step], ret.at[b, ny - step], at_y(step))

    def combine(b):
        for step in range(1, ny):
            rcopy[b, step].wait_recv()
        spread = seltr[b]
        for start, size in tiles(wide):
            value = ret[b, :, :, start:start + size].reshape(count, size)
            out = dot_n(spread, value).reshape(4, tok, size)
            part[4 * b:4 * b + 4, :, start:start + size] = out

    for step in range(1, half + 1):
        if step == 1:
            mcopy[-1].wait_recv()
            mcopy[1].wait_recv()
        for sign, last in ((-1, half), (1, half - 1)):
            if step <= last:
                xcopy[sign * step].wait_recv()
                if step < last:
                    xcopy[sign * (step + 1)] = send(
                        xa.at[place[sign * step]], xa.at[place[sign * (step + 1)]], at_z(-sign)
                    )
        for sign, last in ((-1, half - 1), (1, half)):
            if step <= last:
                dcopy[sign * step].wait_recv()
                if step < last:
                    dcopy[sign * (step + 1)] = send(
                        dya.at[place[sign * step]], dya.at[place[sign * (step + 1)]], at_z(-sign)
                    )
        if step % 2 == 0:
            dispatch(step // 2 - 1)
        if step == max(1, half // 4 + 1):
            near_weights()
        if step == max(1, half // 2):
            far_weights()
        if step == half - 2 and step > 3:
            all_weights()
            compute(0)
        if step == half - 1 and step > 3:
            compute(1)
    if half <= 5:
        all_weights()
    for b in range(2 if half > 5 else 0, batches):
        compute(b)

    act_all = act[...].reshape(batches * count, nx * hid)
    act_t = act_all.T
    for start, size in tiles(width):
        value = rows[:, :, block:2 * block, start:start + size].reshape(batches * count, size)
        out = dot_n(act_t, value).reshape(nx, 2, half_hid, size)
        gmine[:, :, start:start + size] = out[:, 0]
        gsend[:, :, start:start + size] = out[:, 1].astype(BF16)
    gcopy = send(gsend, gpart, partner)

    for b in range(batches):
        combine(b)
        if b == max(0, batches - 2):
            gcopy.wait_recv()
            for rel in range(nx):
                total = gmine[rel] + gpart[rel].astype(F32)
                if rel:
                    ssend[rel] = total.astype(BF16)
                else:
                    gmine[0] = total
            scopy = [send(ssend.at[rel], srecv.at[nx - rel], at_x(rel)) for rel in range(1, nx)]

    cols = (pl.ds(0, mid), pl.ds(mid, wide - mid))
    fcopy, bcopy = {}, {}
    for dist in range(half, 0, -1):
        for col in (0, 1):
            for sign, sends, recvs, copies in ((1, fsend, frecv, fcopy), (-1, bsend, brecv, bcopy)):
                first = half if (col == 0) == (sign == 1) else half - 1
                if dist > first:
                    continue
                value = part[place[sign * dist], :, cols[col]]
                if dist < first:
                    copies[col, dist].wait_recv()
                    value = value + recvs[dist, :, cols[col]].astype(F32)
                sends[dist, :, cols[col]] = value.astype(BF16)
                copies[col, dist - 1] = send(
                    sends.at[dist, :, cols[col]], recvs.at[dist - 1, :, cols[col]], at_z(sign)
                )
        if dist == max(1, half // 2 - 1):
            total = gmine[0]
            for rel in range(1, nx):
                scopy[rel - 1].wait_recv()
            for rel in range(1, nx):
                total = total + srecv[rel].astype(F32)
            gfin[...] = total
            grad_ref[core] = total
            fin = send(gfin, gother, partner)
    fin.wait_recv()
    grad_ref[1 - core] = gother[...]
    for col in (0, 1):
        fcopy[col, 0].wait_recv()
        bcopy[col, 0].wait_recv()
    final = part[0] + frecv[0].astype(F32) + brecv[0].astype(F32)
    dtok_ref[...] = final[:, 0:width].astype(BF16)
    probs = final[:, width:wide]
    slot = lax.broadcasted_iota(jnp.int32, (tok, 4), 1)
    result = jnp.zeros((tok, 4), F32)
    for k in range(4):
        value = jnp.sum(jnp.where(lane == ids_ref[:, k:k + 1], probs, 0.0), axis=1, keepdims=True)
        result = jnp.where(slot == k, value / rw_ref[:, k:k + 1].astype(F32), result)
    dprob_ref[...] = result.astype(BF16)
    for copy in started:
        copy.wait_send()


def local(sizes, tokens, upstream, expert_ids, route_weight, gate_weight, up_weight, down_weight):
    nx, ny, nz = sizes
    tok, width = tokens.shape
    hid = gate_weight.shape[1]
    half_hid, hidden = hid // 2, hid * nx
    half, batches = nz // 2, nz // 4
    wide, block = width + LANES, 4 * CAP
    count = ny * block
    vmem = pl.BlockSpec(memory_space=pltpu.VMEM)
    copies = 512
    d_tokens, d_probs, grad = pl.pallas_call(
        functools.partial(kernel, sizes),
        out_shape=(
            jax.ShapeDtypeStruct((tok, width), BF16),
            jax.ShapeDtypeStruct((tok, 4), BF16),
            jax.ShapeDtypeStruct((2, half_hid, width), F32),
        ),
        in_specs=[vmem] * 7,
        out_specs=(vmem, vmem, vmem),
        scratch_shapes=[
            pltpu.VMEM((tok, LANES), BF16),
            pltpu.VMEM((nz, tok, wide), BF16),
            pltpu.VMEM((nz, tok, width), BF16),
            pltpu.VMEM((batches, 4 * tok, count), BF16),
            pltpu.VMEM((batches, ny, 2 * block, width), BF16),
            pltpu.VMEM((batches, ny, 2 * block, width), BF16),
            pltpu.VMEM((3, nx, 2, half_hid, width), BF16),
            pltpu.VMEM((batches, count, hidden), BF16),
            pltpu.VMEM((batches, ny, block, wide), BF16),
            pltpu.VMEM((batches, ny, block, wide), BF16),
            pltpu.VMEM((nz, tok, wide), F32),
            pltpu.VMEM((half + 1, tok, wide), BF16),
            pltpu.VMEM((half, tok, wide), BF16),
            pltpu.VMEM((half + 1, tok, wide), BF16),
            pltpu.VMEM((half, tok, wide), BF16),
            pltpu.VMEM((nx, half_hid, width), F32),
            pltpu.VMEM((nx, half_hid, width), BF16),
            pltpu.VMEM((nx, half_hid, width), BF16),
            pltpu.VMEM((nx, half_hid, width), BF16),
            pltpu.VMEM((nx, half_hid, width), BF16),
            pltpu.VMEM((half_hid, width), F32),
            pltpu.VMEM((half_hid, width), F32),
            pltpu.SemaphoreType.DMA((160,)),
            pltpu.SemaphoreType.DMA((160,)),
        ],
        compiler_params=pltpu.CompilerParams(
            collective_id=0, has_side_effects=True, vmem_limit_bytes=58 << 20
        ),
    )(
        tokens, upstream, expert_ids, route_weight,
        gate_weight[0], up_weight[0], down_weight[0],
    )
    return d_tokens, d_probs, grad.reshape(1, hid, width)


def build(mesh, ny):
    sizes = (mesh.shape["dp"], ny, mesh.shape["ep"] // ny)
    flat = P(("rep", "ep", "dp"), None)
    split = P("ep", "dp", None)
    return jax.shard_map(
        functools.partial(local, sizes),
        mesh=mesh,
        in_specs=(flat, flat, flat, flat, split, split, split),
        out_specs=(flat, flat, split),
        check_vma=False,
    )


def solution(mesh):
    return build(mesh, 4)
```

```python
import functools

import jax
import jax.numpy as jnp
from jax import lax
from jax.experimental import pallas as pl
from jax.experimental.pallas import tpu as pltpu
from jax.sharding import PartitionSpec as P

MESH = pl.DeviceIdType.MESH
F32, BF16 = jnp.float32, jnp.bfloat16
CAP = 4
LANES = 128
TILE = 512


def dot_t(left, right):
    return lax.dot_general(left, right, (((1,), (1,)), ((), ())), preferred_element_type=F32)


def dot_n(left, right):
    return lax.dot_general(left, right, (((1,), (0,)), ((), ())), preferred_element_type=F32)


def tiles(width):
    return [(start, min(TILE, width - start)) for start in range(0, width, TILE)]


def kernel(
    sizes, tok_ref, ups_ref, ids_ref, rw_ref, gate_ref, up_ref, down_ref,
    total_ref, grad_ref,
    meta, xa, dya, seltr, stage, rows, weights, act, dgate, dup, dxs, ret, part,
    fsend, frecv, bsend, brecv, gacc, gsend, gpart, ssend, srecv, gfin, gother,
    send_sem, recv_sem, local_sem,
):
    nx, ny, nz = sizes
    tok, width = tok_ref.shape
    hid = gate_ref.shape[0]
    half_hid = hid // 2
    hidden = nx * hid
    half = nz // 2
    batches = nz // 4
    pairs = nz // 2
    wide = width + LANES
    mid = width // 2
    core, ep, dp = lax.axis_index("rep"), lax.axis_index("ep"), lax.axis_index("dp")
    z, y = ep // ny, lax.rem(ep, ny)

    def at_z(step):
        return (core, lax.rem(z + step + nz, nz) * ny + y, dp)

    def at_y(step):
        return (core, z * ny + lax.rem(y + step, ny), dp)

    def at_x(step):
        return (core, ep, lax.rem(dp + step, nx))

    partner = (1 - core, ep, dp)

    order = [0]
    for step in range(1, half):
        order += [-step, step]
    order.append(half)
    place = {delta: index for index, delta in enumerate(order)}
    place[-half] = place[half]

    started = []

    def send(src, dst, device):
        index = len(started)
        copy = pltpu.make_async_remote_copy(
            src_ref=src, dst_ref=dst, send_sem=send_sem.at[index],
            recv_sem=recv_sem.at[index], device_id=device, device_id_type=MESH,
        )
        copy.start()
        started.append(copy)
        return copy

    shard_refs = (gate_ref, up_ref, down_ref)
    mine = pl.ds(pl.multiple_of(core * half_hid, half_hid), half_hid)
    theirs = pl.ds(pl.multiple_of((1 - core) * half_hid, half_hid), half_hid)
    loads = [(tok_ref, xa.at[0, :, pl.ds(0, width)]), (ups_ref, dya.at[0])]
    for index, ref in enumerate(shard_refs):
        loads.append((ref.at[mine], weights.at[index, 0, 0]))
        loads.append((ref.at[theirs], weights.at[index, 0, 1]))
    loads = [
        pltpu.make_async_copy(src, dst, local_sem.at[index])
        for index, (src, dst) in enumerate(loads)
    ]
    for copy in loads:
        copy.start()

    barrier = pltpu.get_barrier_semaphore()
    peers = [at_z(1), at_z(-1), partner]
    peers += [at_y(step) for step in range(1, ny)]
    peers += [at_x(step) for step in range(1, nx)]
    for peer in peers:
        pl.semaphore_signal(barrier, inc=1, device_id=peer, device_id_type=MESH)
    pl.semaphore_wait(barrier, len(peers))

    xcopy, dcopy, mcopy = {}, {}, {}
    for sign in (-1, 1):
        xcopy[sign] = send(tok_ref, xa.at[place[sign], :, pl.ds(0, width)], at_z(-sign))

    name = lax.broadcasted_iota(jnp.int32, (LANES, tok), 0)
    scales = rw_ref[...].astype(F32)
    routed = jnp.zeros((LANES, tok), F32)
    scale = jnp.zeros((LANES, tok), F32)
    for k in range(4):
        chosen_name = ids_ref[k:k + 1, :]
        routed = routed + jnp.where(name == chosen_name, 1.0, 0.0)
        scale = scale + jnp.where(name == chosen_name + 64, scales[k:k + 1, :], 0.0)
    first = lax.broadcasted_iota(jnp.int32, (tok, tok), 0)
    second = lax.broadcasted_iota(jnp.int32, (tok, tok), 1)
    upper = jnp.where(first < second, 1.0, 0.0).astype(BF16)
    same = jnp.where(first == second, 1.0, 0.0).astype(BF16)
    rank = routed * (dot_n(routed.astype(BF16), upper) + 1.0)
    own_meta = dot_t(same, (rank + scale).astype(BF16)).astype(BF16)
    meta[...] = own_meta
    for sign in (-1, 1):
        mcopy[sign] = send(meta, xa.at[place[sign], :, pl.ds(width, LANES)], at_z(-sign))
    for sign in (-1, 1):
        dcopy[sign] = send(ups_ref, dya.at[place[sign]], at_z(-sign))
    xa[0, :, width:wide] = own_meta

    wcopy = {}
    for index, ref in enumerate(shard_refs):
        wcopy[index, nx - 1] = send(ref.at[mine], weights.at[index, nx - 1, 0], at_x(1))
        if nx == 4:
            wcopy[index, 1] = send(ref.at[mine], weights.at[index, 1, 0], at_x(3))
    for copy in loads:
        copy.wait()

    hcopy = []

    def near_weights():
        for index in range(3):
            wcopy[index, nx - 1].wait_recv()
            if nx == 4:
                wcopy[index, 1].wait_recv()
                if index == 1:
                    wcopy[index, 2] = send(weights.at[index, 1, 0], weights.at[index, 2, 0], at_x(3))
                else:
                    wcopy[index, 2] = send(weights.at[index, 3, 0], weights.at[index, 2, 0], at_x(1))
        for index in range(3):
            for rel in ((1, 3) if nx == 4 else (1,)):
                hcopy.append(send(weights.at[index, rel, 0], weights.at[index, rel, 1], partner))

    def far_weights():
        if nx == 4:
            for index in range(3):
                wcopy[index, 2].wait_recv()
                hcopy.append(send(weights.at[index, 2, 0], weights.at[index, 2, 1], partner))

    def all_weights():
        for copy in hcopy:
            copy.wait_recv()

    ycopy = {}
    block = 2 * CAP
    count = ny * block

    def chosen(value, r, c, sources):
        slot = (lax.rem(r, CAP) + 1).astype(F32)
        return (value == slot) & (c // tok == lax.rem(r // CAP, sources))

    def picks(size, row_block):
        row = lax.broadcasted_iota(jnp.int32, (size, LANES), 0)
        col = lax.broadcasted_iota(jnp.int32, (size, LANES), 1)
        expert = z * ny + lax.rem(y + row // row_block, ny)
        pick = jnp.where(col == expert, 1.0, 0.0).astype(BF16)
        pick_w = jnp.where(col == expert + 64, 1.0, 0.0).astype(BF16)
        return pick, pick_w

    def dispatch(p):
        group = xa[2 * p:2 * p + 2, :, width:wide].reshape(2 * tok, LANES)
        pick, pick_w = picks(count, block)
        shape = (count, 2 * tok)
        r, c = (lax.broadcasted_iota(jnp.int32, shape, axis) for axis in (0, 1))
        hit = chosen(dot_t(pick, group), r, c, 2)
        sel = jnp.where(hit, 1.0, 0.0).astype(BF16)
        sel_w = jnp.where(hit, dot_t(pick_w, group), 0.0).astype(BF16)
        for start, size in tiles(width):
            parts = []
            for source, chooser in ((xa, sel), (dya, sel_w)):
                value = source[2 * p:2 * p + 2, :, start:start + size].reshape(2 * tok, size)
                parts.append(dot_n(chooser, value).reshape(ny, block, size))
            out = jnp.concatenate(parts, axis=1).astype(BF16)
            rows[p, 0, :, start:start + size] = out[0]
            stage[p, 1:ny, :, start:start + size] = out[1:ny]
        for step in range(1, ny):
            ycopy[p, step] = send(stage.at[p, step], rows.at[p, ny - step], at_y(step))

    rcopy = {}
    cols = (pl.ds(0, mid), pl.ds(mid, wide - mid))

    def split(value):
        value = value.reshape(2 * ny, 2, block, hidden)
        return value[:, 0], value[:, 1]

    def forward(b):
        for p in (2 * b, 2 * b + 1):
            for step in range(1, ny):
                ycopy[p, step].wait_recv()
        both = rows[2 * b:2 * b + 2].reshape(4 * count, width)
        gate_pre, _ = split(dot_t(both, weights[0].reshape(hidden, width)))
        up_pre, _ = split(dot_t(both, weights[1].reshape(hidden, width)))
        _, d_act = split(dot_t(both, weights[2].reshape(hidden, width)))
        sig = jax.nn.sigmoid(gate_pre)
        silu = gate_pre * sig
        act_rows = (silu * up_pre).astype(BF16).astype(F32)
        act[b] = jnp.concatenate([jnp.zeros_like(act_rows), act_rows], axis=1).reshape(4 * count, hidden).astype(BF16)
        d_gate = d_act * up_pre * sig * (1.0 + gate_pre * (1.0 - sig))
        dgate[...] = d_gate.reshape(2 * count, hidden).astype(BF16)
        dup[...] = (d_act * silu).reshape(2 * count, hidden).astype(BF16)
        prob = jnp.sum(act_rows * d_act, axis=2, keepdims=True)
        here = lax.broadcasted_iota(jnp.int32, (2 * ny, block, LANES), 2) == ep
        give(b, width, LANES, jnp.where(here, prob, 0.0))

    def give(b, start, size, value):
        value = value.reshape(2, ny, block, size)
        value = jnp.concatenate([value[0], value[1]], axis=1).astype(BF16)
        dxs[b, 1:ny, :, start:start + size] = value[1:ny]
        ret[b, 0, :, start:start + size] = value[0]

    def backward(b):
        d_gate, d_up = dgate[...], dup[...]
        done = 0
        for start, size in tiles(width):
            gate_t = weights[0, :, :, :, start:start + size].reshape(hidden, size)
            up_t = weights[1, :, :, :, start:start + size].reshape(hidden, size)
            give(b, start, size, dot_n(d_gate, gate_t) + dot_n(d_up, up_t))
            if done == 0 and start + size >= mid or start + size == width:
                for step in range(1, ny):
                    rcopy[b, done, step] = send(
                        dxs.at[b, step, :, cols[done]], ret.at[b, ny - step, :, cols[done]], at_y(step)
                    )
                done += 1

    def spread(b):
        group = xa[4 * b:4 * b + 4, :, width:wide].reshape(4 * tok, LANES)
        pick, _ = picks(2 * count, 2 * block)
        shape = (4 * tok, 2 * count)
        c, r = (lax.broadcasted_iota(jnp.int32, shape, axis) for axis in (0, 1))
        seltr[b] = jnp.where(chosen(dot_t(group, pick), r, c, 4), 1.0, 0.0).astype(BF16)

    def combine(b, col):
        for step in range(1, ny):
            rcopy[b, col, step].wait_recv()
        low, high = ((0, mid), (mid, wide))[col]
        for start, size in tiles(high - low):
            start += low
            value = ret[b, :, :, start:start + size].reshape(2 * count, size)
            out = dot_n(seltr[b], value).reshape(4, tok, size)
            part[4 * b:4 * b + 4, :, start:start + size] = out

    def grads(b):
        act_t = act[b].T
        for start, size in tiles(width):
            value = rows[2 * b:2 * b + 2, :, :, start:start + size].reshape(4 * count, size)
            out = dot_n(act_t, value).reshape(nx, 2, half_hid, size)
            if b:
                out = out + gacc[:, :, :, start:start + size]
            gacc[:, :, :, start:start + size] = out
            if b == batches - 1:
                gsend[:, :, start:start + size] = out[:, 1].astype(BF16)

    if half == 8:
        table = {
            4: [near_weights], 8: [far_weights], 9: [all_weights],
            10: [lambda: forward(0)], 11: [lambda: backward(0)],
            12: [lambda: forward(1)], 13: [lambda: backward(1)],
            14: [lambda: grads(0)], 15: [lambda: grads(1)],
            17: [lambda: forward(2), lambda: backward(2), lambda: grads(2)],
        }
    else:
        table = {2 * half + 1: [near_weights, far_weights, all_weights]}
        for b in range(batches - 1):
            table[2 * half + 1] += [
                functools.partial(forward, b), functools.partial(backward, b), functools.partial(grads, b)
            ]

    for step in range(1, half + 1):
        if step == 1:
            mcopy[-1].wait_recv()
            mcopy[1].wait_recv()
        for moving, copies, ends, slot in (
            (xa, xcopy, (half, half - 1), 2 * step), (dya, dcopy, (half - 1, half), 2 * step + 1),
        ):
            for sign, last in zip((-1, 1), ends):
                if step <= last:
                    copies[sign * step].wait_recv()
                    if step < last:
                        copies[sign * (step + 1)] = send(
                            moving.at[place[sign * step]], moving.at[place[sign * (step + 1)]], at_z(-sign)
                        )
            if slot == 2 * step + 1:
                dispatch(step - 1)
            for task in table.get(slot, ()):
                task()

    last = batches - 1
    forward(last)
    backward(last)
    grads(last)
    gcopy = send(gsend, gpart, partner)
    for b in range(batches):
        spread(b)
    for b in range(batches - 1):
        for col in (0, 1):
            combine(b, col)

    def pair_sum():
        gcopy.wait_recv()
        for rel in range(nx):
            total = gacc[rel, 0] + gpart[rel].astype(F32)
            if rel:
                ssend[rel] = total.astype(BF16)
            else:
                gacc[0, 0] = total
        return [send(ssend.at[rel], srecv.at[nx - rel], at_x(rel)) for rel in range(1, nx)]

    fcopy, bcopy = {}, {}
    for dist in range(half, 0, -1):
        for col in (0, 1):
            if dist == half:
                combine(last, col)
            for sign, sends, recvs, copies in ((1, fsend, frecv, fcopy), (-1, bsend, brecv, bcopy)):
                first = half if (col == 0) == (sign == 1) else half - 1
                if dist > first:
                    continue
                value = part[place[sign * dist], :, cols[col]]
                if dist < first:
                    copies[col, dist].wait_recv()
                    value = value + recvs[dist, :, cols[col]].astype(F32)
                sends[dist, :, cols[col]] = value.astype(BF16)
                copies[col, dist - 1] = send(
                    sends.at[dist, :, cols[col]], recvs.at[dist - 1, :, cols[col]], at_z(sign)
                )
        if dist == half:
            scopy = pair_sum()
        if dist == max(1, half // 4):
            total = gacc[0, 0]
            for rel in range(1, nx):
                scopy[rel - 1].wait_recv()
            for rel in range(1, nx):
                total = total + srecv[rel].astype(F32)
            gfin[...] = total
            grad_ref[core] = total
            fin = send(gfin, gother, partner)
    fin.wait_recv()
    grad_ref[1 - core] = gother[...]
    for col in (0, 1):
        fcopy[col, 0].wait_recv()
        bcopy[col, 0].wait_recv()
    total_ref[...] = part[0] + frecv[0].astype(F32) + brecv[0].astype(F32)
    for copy in started:
        copy.wait_send()


def finish(total_any, halves_ref, ids_ref, rw_ref, dtok_ref, dprob_ref, grad_ref, total_ref, sem):
    tok, width = dtok_ref.shape
    grad_copy = pltpu.make_async_copy(halves_ref, grad_ref, sem.at[0])
    total_copy = pltpu.make_async_copy(total_any, total_ref, sem.at[1])
    total_copy.start()
    grad_copy.start()
    total_copy.wait()
    dtok_ref[...] = total_ref[:, 0:width].astype(BF16)
    probs = total_ref[:, width:width + LANES].astype(BF16)
    name = lax.broadcasted_iota(jnp.int32, (LANES, LANES), 0)
    other = lax.broadcasted_iota(jnp.int32, (LANES, LANES), 1)
    same = jnp.where(name == other, 1.0, 0.0).astype(BF16)
    probs = dot_t(same, probs)
    name = lax.broadcasted_iota(jnp.int32, (LANES, tok), 0)
    slot = lax.broadcasted_iota(jnp.int32, (4, tok), 0)
    values = jnp.zeros((4, tok), F32)
    for k in range(4):
        value = jnp.sum(jnp.where(name == ids_ref[k:k + 1, :], probs, 0.0), axis=0, keepdims=True)
        values = jnp.where(slot == k, value, values)
    dprob_ref[...] = (values / rw_ref[...].astype(F32)).astype(BF16)
    grad_copy.wait()


def local(sizes, tokens, upstream, expert_ids, route_weight, gate_weight, up_weight, down_weight):
    nx, ny, nz = sizes
    tok, width = tokens.shape
    hid = gate_weight.shape[1]
    half_hid, hidden = hid // 2, hid * nx
    half, batches = nz // 2, nz // 4
    wide, block = width + LANES, 4 * CAP
    count = ny * block
    vmem = pl.BlockSpec(memory_space=pltpu.VMEM)
    hbm = pl.BlockSpec(memory_space=pltpu.HBM)
    anywhere = pl.BlockSpec(memory_space=pl.ANY)
    ids, scales = expert_ids.T, route_weight.T

    def stay(value):
        return pltpu.with_memory_space_constraint(value, pltpu.HBM)

    total, halves = pl.pallas_call(
        functools.partial(kernel, sizes),
        out_shape=(
            jax.ShapeDtypeStruct((tok, wide), F32),
            jax.ShapeDtypeStruct((2, half_hid, width), F32),
        ),
        in_specs=[hbm, hbm, vmem, vmem, hbm, hbm, hbm],
        out_specs=(vmem, vmem),
        scratch_shapes=[
            pltpu.VMEM((tok, LANES), BF16),
            pltpu.VMEM((nz, tok, wide), BF16),
            pltpu.VMEM((nz, tok, width), BF16),
            pltpu.VMEM((batches, 4 * tok, count), BF16),
            pltpu.VMEM((nz // 2, ny, block, width), BF16),
            pltpu.VMEM((nz // 2, ny, block, width), BF16),
            pltpu.VMEM((3, nx, 2, half_hid, width), BF16),
            pltpu.VMEM((batches, 2 * count, hidden), BF16),
            pltpu.VMEM((count, hidden), BF16),
            pltpu.VMEM((count, hidden), BF16),
            pltpu.VMEM((batches, ny, block, wide), BF16),
            pltpu.VMEM((batches, ny, block, wide), BF16),
            pltpu.VMEM((nz, tok, wide), F32),
            pltpu.VMEM((half + 1, tok, wide), BF16),
            pltpu.VMEM((half, tok, wide), BF16),
            pltpu.VMEM((half + 1, tok, wide), BF16),
            pltpu.VMEM((half, tok, wide), BF16),
            pltpu.VMEM((nx, 2, half_hid, width), F32),
            pltpu.VMEM((nx, half_hid, width), BF16),
            pltpu.VMEM((nx, half_hid, width), BF16),
            pltpu.VMEM((nx, half_hid, width), BF16),
            pltpu.VMEM((nx, half_hid, width), BF16),
            pltpu.VMEM((half_hid, width), F32),
            pltpu.VMEM((half_hid, width), F32),
            pltpu.SemaphoreType.DMA((192,)),
            pltpu.SemaphoreType.DMA((192,)),
            pltpu.SemaphoreType.DMA((8,)),
        ],
        compiler_params=pltpu.CompilerParams(
            collective_id=0, has_side_effects=True, vmem_limit_bytes=48 << 20
        ),
    )(
        stay(tokens), stay(upstream), ids, scales,
        stay(gate_weight[0]), stay(up_weight[0]), stay(down_weight[0]),
    )
    d_tokens, d_probs, grad = pl.pallas_call(
        finish,
        out_shape=(
            jax.ShapeDtypeStruct((tok, width), BF16),
            jax.ShapeDtypeStruct((4, tok), BF16),
            jax.ShapeDtypeStruct((2, half_hid, width), F32),
        ),
        in_specs=[anywhere, anywhere, vmem, vmem],
        out_specs=(vmem, vmem, anywhere),
        scratch_shapes=[pltpu.VMEM((tok, wide), F32), pltpu.SemaphoreType.DMA((2,))],
        compiler_params=pltpu.CompilerParams(vmem_limit_bytes=8 << 20),
    )(total, halves, ids, scales)
    return d_tokens, d_probs.T, grad.reshape(1, hid, width)


def build(mesh, ny):
    sizes = (mesh.shape["dp"], ny, mesh.shape["ep"] // ny)
    flat = P(("rep", "ep", "dp"), None)
    split = P("ep", "dp", None)
    return jax.shard_map(
        functools.partial(local, sizes),
        mesh=mesh,
        in_specs=(flat, flat, flat, flat, split, split, split),
        out_specs=(flat, flat, split),
        check_vma=False,
    )


def solution(mesh):
    return build(mesh, 4)
```

```python
import functools

import jax
import jax.numpy as jnp
from jax import lax
from jax.experimental import pallas as pl
from jax.experimental.pallas import tpu as pltpu
from jax.sharding import PartitionSpec as P

MESH = pl.DeviceIdType.MESH
F32, BF16 = jnp.float32, jnp.bfloat16
CAP = 4
LANES = 128
TILE = 512


def dot_t(left, right):
    return lax.dot_general(left, right, (((1,), (1,)), ((), ())), preferred_element_type=F32)


def dot_n(left, right):
    return lax.dot_general(left, right, (((1,), (0,)), ((), ())), preferred_element_type=F32)


def tiles(width):
    return [(start, min(TILE, width - start)) for start in range(0, width, TILE)]


def kernel(
    sizes, tok_ref, ups_ref, ids_ref, rw_ref, gate_ref, up_ref, down_ref,
    total_ref, grad_ref,
    meta, xa, dya, seltr, stage, rows, weights, act, dgate, dup, dxs, ret, part,
    fsend, frecv, bsend, brecv, gacc, gsend, gpart, ssend, srecv, gfin, gother,
    ids_own, rw_own, send_sem, recv_sem, local_sem,
):
    nx, ny, nz = sizes
    tok, width = tok_ref.shape
    hid = gate_ref.shape[0]
    half_hid = hid // 2
    hidden = nx * hid
    half = nz // 2
    batches = nz // 4
    pairs = nz // 2
    wide = width + LANES
    core, ep, dp = lax.axis_index("rep"), lax.axis_index("ep"), lax.axis_index("dp")
    z, y = ep // ny, lax.rem(ep, ny)

    def at_z(step):
        return (core, lax.rem(z + step + nz, nz) * ny + y, dp)

    def at_y(step):
        return (core, z * ny + lax.rem(y + step, ny), dp)

    def at_x(step):
        return (core, ep, lax.rem(dp + step, nx))

    partner = (1 - core, ep, dp)

    order = [0]
    for step in range(1, half):
        order += [-step, step]
    order.append(half)
    place = {delta: index for index, delta in enumerate(order)}
    place[-half] = place[half]

    started = []

    def send(src, dst, device):
        index = len(started)
        copy = pltpu.make_async_remote_copy(
            src_ref=src, dst_ref=dst, send_sem=send_sem.at[index],
            recv_sem=recv_sem.at[index], device_id=device, device_id_type=MESH,
        )
        copy.start()
        started.append(copy)
        return copy

    shard_refs = (gate_ref, up_ref, down_ref)
    mine = pl.ds(pl.multiple_of(core * half_hid, half_hid), half_hid)
    theirs = pl.ds(pl.multiple_of((1 - core) * half_hid, half_hid), half_hid)
    loads = [(ids_ref, ids_own), (rw_ref, rw_own), (tok_ref, xa.at[0, :, pl.ds(0, width)]), (ups_ref, dya.at[0])]
    for index, ref in enumerate(shard_refs):
        loads.append((ref.at[mine], weights.at[index, 0, 0]))
        loads.append((ref.at[theirs], weights.at[index, 0, 1]))
    loads = [
        pltpu.make_async_copy(src, dst, local_sem.at[index])
        for index, (src, dst) in enumerate(loads)
    ]
    for copy in loads:
        copy.start()

    barrier = pltpu.get_barrier_semaphore()
    peers = [at_z(1), at_z(-1), partner]
    peers += [at_y(step) for step in range(1, ny)]
    peers += [at_x(step) for step in range(1, nx)]
    for peer in peers:
        pl.semaphore_signal(barrier, inc=1, device_id=peer, device_id_type=MESH)
    loads[0].wait()
    loads[1].wait()
    pl.semaphore_wait(barrier, len(peers))

    xcopy, dcopy, mcopy = {}, {}, {}

    def first_x(sign):
        xcopy[sign] = send(tok_ref, xa.at[place[sign], :, pl.ds(0, width)], at_z(-sign))

    def first_d(sign):
        dcopy[sign] = send(ups_ref, dya.at[place[sign]], at_z(-sign))

    def first_m(sign):
        mcopy[sign] = send(meta, xa.at[place[sign], :, pl.ds(width, LANES)], at_z(-sign))

    first_x(-1)
    first_d(1)

    name = lax.broadcasted_iota(jnp.int32, (LANES, tok), 0)
    scales = rw_own[...].astype(F32)
    routed = jnp.zeros((LANES, tok), F32)
    scale = jnp.zeros((LANES, tok), F32)
    for k in range(4):
        chosen_name = ids_own[k:k + 1, :]
        routed = routed + jnp.where(name == chosen_name, 1.0, 0.0)
        scale = scale + jnp.where(name == chosen_name + 64, scales[k:k + 1, :], 0.0)
    first = lax.broadcasted_iota(jnp.int32, (tok, tok), 0)
    second = lax.broadcasted_iota(jnp.int32, (tok, tok), 1)
    upper = jnp.where(first < second, 1.0, 0.0).astype(BF16)
    same = jnp.where(first == second, 1.0, 0.0).astype(BF16)
    rank = routed * (dot_n(routed.astype(BF16), upper) + 1.0)
    own_meta = dot_t(same, (rank + scale).astype(BF16)).astype(BF16)
    meta[...] = own_meta
    first_m(-1)
    first_x(1)
    first_m(1)
    first_d(-1)
    xa[0, :, width:wide] = own_meta

    wcopy = {}
    for index, ref in enumerate(shard_refs):
        wcopy[index, nx - 1] = send(ref.at[mine], weights.at[index, nx - 1, 0], at_x(1))
        if nx == 4:
            wcopy[index, 1] = send(ref.at[mine], weights.at[index, 1, 0], at_x(3))
    for copy in loads[2:]:
        copy.wait()

    hcopy = []

    def near_weights():
        for index in range(3):
            wcopy[index, nx - 1].wait_recv()
            if nx == 4:
                wcopy[index, 1].wait_recv()
                if index == 1:
                    wcopy[index, 2] = send(weights.at[index, 1, 0], weights.at[index, 2, 0], at_x(3))
                else:
                    wcopy[index, 2] = send(weights.at[index, 3, 0], weights.at[index, 2, 0], at_x(1))
        for index in range(3):
            for rel in ((1, 3) if nx == 4 else (1,)):
                hcopy.append(send(weights.at[index, rel, 0], weights.at[index, rel, 1], partner))

    def far_weights():
        if nx == 4:
            for index in range(3):
                wcopy[index, 2].wait_recv()
                hcopy.append(send(weights.at[index, 2, 0], weights.at[index, 2, 1], partner))

    def all_weights():
        for copy in hcopy:
            copy.wait_recv()

    ycopy = {}
    block = 2 * CAP
    count = ny * block

    def chosen(value, r, c, sources):
        slot = (lax.rem(r, CAP) + 1).astype(F32)
        return (value == slot) & (c // tok == lax.rem(r // CAP, sources))

    def picks(size, row_block):
        row = lax.broadcasted_iota(jnp.int32, (size, LANES), 0)
        col = lax.broadcasted_iota(jnp.int32, (size, LANES), 1)
        expert = z * ny + lax.rem(y + row // row_block, ny)
        pick = jnp.where(col == expert, 1.0, 0.0).astype(BF16)
        pick_w = jnp.where(col == expert + 64, 1.0, 0.0).astype(BF16)
        return pick, pick_w

    def dispatch(p):
        group = xa[2 * p:2 * p + 2, :, width:wide].reshape(2 * tok, LANES)
        pick, pick_w = picks(count, block)
        shape = (count, 2 * tok)
        r, c = (lax.broadcasted_iota(jnp.int32, shape, axis) for axis in (0, 1))
        hit = chosen(dot_t(pick, group), r, c, 2)
        sel = jnp.where(hit, 1.0, 0.0).astype(BF16)
        sel_w = jnp.where(hit, dot_t(pick_w, group), 0.0).astype(BF16)
        for start, size in tiles(width):
            parts = []
            for source, chooser in ((xa, sel), (dya, sel_w)):
                value = source[2 * p:2 * p + 2, :, start:start + size].reshape(2 * tok, size)
                parts.append(dot_n(chooser, value).reshape(ny, block, size))
            out = jnp.concatenate(parts, axis=1).astype(BF16)
            rows[p, 0, :, start:start + size] = out[0]
            stage[p, 1:ny, :, start:start + size] = out[1:ny]
        for step in range(1, ny):
            ycopy[p, step] = send(stage.at[p, step], rows.at[p, ny - step], at_y(step))

    rcopy = {}
    edges = [(width // 4 * c, width // 4 if c < 3 else wide - width // 4 * 3) for c in range(4)]
    cols = [pl.ds(start, size) for start, size in edges]

    def split(value):
        value = value.reshape(2 * ny, 2, block, hidden)
        return value[:, 0], value[:, 1]

    def forward(b):
        for p in (2 * b, 2 * b + 1):
            for step in range(1, ny):
                ycopy[p, step].wait_recv()
        both = rows[2 * b:2 * b + 2].reshape(4 * count, width)
        gate_pre, _ = split(dot_t(both, weights[0].reshape(hidden, width)))
        up_pre, _ = split(dot_t(both, weights[1].reshape(hidden, width)))
        _, d_act = split(dot_t(both, weights[2].reshape(hidden, width)))
        sig = jax.nn.sigmoid(gate_pre)
        silu = gate_pre * sig
        act_rows = (silu * up_pre).astype(BF16).astype(F32)
        act[b] = jnp.concatenate([jnp.zeros_like(act_rows), act_rows], axis=1).reshape(4 * count, hidden).astype(BF16)
        d_gate = d_act * up_pre * sig * (1.0 + gate_pre * (1.0 - sig))
        dgate[...] = d_gate.reshape(2 * count, hidden).astype(BF16)
        dup[...] = (d_act * silu).reshape(2 * count, hidden).astype(BF16)
        prob = jnp.sum(act_rows * d_act, axis=2, keepdims=True)
        here = lax.broadcasted_iota(jnp.int32, (2 * ny, block, LANES), 2) == ep
        give(b, width, LANES, jnp.where(here, prob, 0.0))

    def give(b, start, size, value):
        value = value.reshape(2, ny, block, size)
        value = jnp.concatenate([value[0], value[1]], axis=1).astype(BF16)
        dxs[b, 1:ny, :, start:start + size] = value[1:ny]
        ret[b, 0, :, start:start + size] = value[0]

    def backward(b):
        d_gate, d_up = dgate[...], dup[...]
        for col in range(4):
            start, size = width // 4 * col, width // 4
            gate_t = weights[0, :, :, :, start:start + size].reshape(hidden, size)
            up_t = weights[1, :, :, :, start:start + size].reshape(hidden, size)
            give(b, start, size, dot_n(d_gate, gate_t) + dot_n(d_up, up_t))
            if b == batches - 1:
                for step in range(1, ny):
                    rcopy[b, col, step] = send(
                        dxs.at[b, step, :, cols[col]], ret.at[b, ny - step, :, cols[col]], at_y(step)
                    )
        if b < batches - 1:
            for step in range(1, ny):
                rcopy[b, 0, step] = send(dxs.at[b, step], ret.at[b, ny - step], at_y(step))

    def spread(b):
        group = xa[4 * b:4 * b + 4, :, width:wide].reshape(4 * tok, LANES)
        pick, _ = picks(2 * count, 2 * block)
        shape = (4 * tok, 2 * count)
        c, r = (lax.broadcasted_iota(jnp.int32, shape, axis) for axis in (0, 1))
        seltr[b] = jnp.where(chosen(dot_t(group, pick), r, c, 4), 1.0, 0.0).astype(BF16)

    def combine(b, col):
        if (b, col, ny - 1) in rcopy:
            for step in range(1, ny):
                rcopy[b, col, step].wait_recv()
        start, size = edges[col]
        value = ret[b, :, :, start:start + size].reshape(2 * count, size)
        part[4 * b:4 * b + 4, :, start:start + size] = dot_n(seltr[b], value).reshape(4, tok, size)

    def grads(b):
        act_t = act[b].T
        for start, size in tiles(width):
            value = rows[2 * b:2 * b + 2, :, :, start:start + size].reshape(4 * count, size)
            out = dot_n(act_t, value).reshape(nx, 2, half_hid, size)
            if b:
                out = out + gacc[:, :, :, start:start + size]
            gacc[:, :, :, start:start + size] = out
            if b == batches - 1:
                gsend[:, :, start:start + size] = out[:, 1].astype(BF16)

    if half == 8:
        table = {
            4: [near_weights], 8: [far_weights], 9: [all_weights],
            10: [lambda: forward(0)], 11: [lambda: backward(0)],
            12: [lambda: forward(1)], 13: [lambda: backward(1)],
            14: [lambda: grads(0)], 15: [lambda: grads(1)],
            17: [lambda: forward(2), lambda: backward(2), lambda: grads(2)],
        }
    else:
        table = {2 * half + 1: [near_weights, far_weights, all_weights]}
        for b in range(batches - 1):
            table[2 * half + 1] += [
                functools.partial(forward, b), functools.partial(backward, b), functools.partial(grads, b)
            ]

    for step in range(1, half + 1):
        for slot, routes in (
            (2 * step, ((xa, xcopy, -1, half), (dya, dcopy, 1, half))),
            (2 * step + 1, ((dya, dcopy, -1, half - 1), (xa, xcopy, 1, half - 1))),
        ):
            for moving, copies, sign, last in routes:
                if step <= last:
                    copies[sign * step].wait_recv()
                    if step == 1 and moving is xa:
                        mcopy[sign].wait_recv()
                    if step < last:
                        copies[sign * (step + 1)] = send(
                            moving.at[place[sign * step]], moving.at[place[sign * (step + 1)]], at_z(-sign)
                        )
            if slot == 2 * step + 1:
                dispatch(step - 1)
            for task in table.get(slot, ()):
                task()

    last = batches - 1
    forward(last)
    backward(last)
    grads(last)
    gcopy = send(gsend, gpart, partner)
    for b in range(batches):
        spread(b)
    for b in range(batches - 1):
        for col in range(4):
            combine(b, col)

    def pair_sum():
        gcopy.wait_recv()
        for rel in range(nx):
            total = gacc[rel, 0] + gpart[rel].astype(F32)
            if rel:
                ssend[rel] = total.astype(BF16)
            else:
                gacc[0, 0] = total
        return [send(ssend.at[rel], srecv.at[nx - rel], at_x(rel)) for rel in range(1, nx)]

    chain = {}

    def relay(col, sign, dist):
        sends, recvs = (fsend, frecv) if sign == 1 else (bsend, brecv)
        value = part[place[sign * dist], :, cols[col]]
        if (col, sign, dist) in chain:
            chain[col, sign, dist].wait_recv()
            value = value + recvs[dist, :, cols[col]].astype(F32)
        sends[dist, :, cols[col]] = value.astype(BF16)
        chain[col, sign, dist - 1] = send(
            sends.at[dist, :, cols[col]], recvs.at[dist - 1, :, cols[col]], at_z(sign)
        )

    for turn in range(half):
        for col in range(4):
            if turn == 0:
                combine(last, col)
            long = 1 if col % 2 == 0 else -1
            relay(col, long, half - turn)
            if turn < half - 1:
                relay(col, -long, half - 1 - turn)
        if turn == 0:
            scopy = pair_sum()
        if turn == max(0, half - 3):
            total = gacc[0, 0]
            for rel in range(1, nx):
                scopy[rel - 1].wait_recv()
            for rel in range(1, nx):
                total = total + srecv[rel].astype(F32)
            gfin[...] = total
            grad_ref[core] = total
            fin = send(gfin, gother, partner)
    fin.wait_recv()
    grad_ref[1 - core] = gother[...]
    for col in range(4):
        chain[col, 1, 0].wait_recv()
        chain[col, -1, 0].wait_recv()
        start, size = edges[col]
        total_ref[:, start:start + size] = (
            part[0, :, start:start + size]
            + frecv[0, :, start:start + size].astype(F32)
            + brecv[0, :, start:start + size].astype(F32)
        )
    for copy in started:
        copy.wait_send()


def finish(total_any, halves_ref, ids_any, rw_any, dtok_ref, dprob_ref, grad_ref, total_ref, ids_ref, rw_ref, sem):
    tok, width = dtok_ref.shape
    grad_copy = pltpu.make_async_copy(halves_ref, grad_ref, sem.at[0])
    total_copy = pltpu.make_async_copy(total_any, total_ref, sem.at[1])
    ids_copy = pltpu.make_async_copy(ids_any, ids_ref, sem.at[2])
    rw_copy = pltpu.make_async_copy(rw_any, rw_ref, sem.at[3])
    for copy in (ids_copy, rw_copy, total_copy, grad_copy):
        copy.start()
    total_copy.wait()
    dtok_ref[...] = total_ref[:, 0:width].astype(BF16)
    probs = total_ref[:, width:width + LANES].astype(BF16)
    name = lax.broadcasted_iota(jnp.int32, (LANES, LANES), 0)
    other = lax.broadcasted_iota(jnp.int32, (LANES, LANES), 1)
    same = jnp.where(name == other, 1.0, 0.0).astype(BF16)
    probs = dot_t(same, probs)
    ids_copy.wait()
    rw_copy.wait()
    name = lax.broadcasted_iota(jnp.int32, (LANES, tok), 0)
    slot = lax.broadcasted_iota(jnp.int32, (4, tok), 0)
    values = jnp.zeros((4, tok), F32)
    for k in range(4):
        value = jnp.sum(jnp.where(name == ids_ref[k:k + 1, :], probs, 0.0), axis=0, keepdims=True)
        values = jnp.where(slot == k, value, values)
    dprob_ref[...] = (values / rw_ref[...].astype(F32)).astype(BF16)
    grad_copy.wait()


def local(sizes, tokens, upstream, expert_ids, route_weight, gate_weight, up_weight, down_weight):
    nx, ny, nz = sizes
    tok, width = tokens.shape
    hid = gate_weight.shape[1]
    half_hid, hidden = hid // 2, hid * nx
    half, batches = nz // 2, nz // 4
    wide, block = width + LANES, 4 * CAP
    count = ny * block
    vmem = pl.BlockSpec(memory_space=pltpu.VMEM)
    hbm = pl.BlockSpec(memory_space=pltpu.HBM)
    anywhere = pl.BlockSpec(memory_space=pl.ANY)
    ids, scales = expert_ids.T, route_weight.T

    def stay(value):
        return pltpu.with_memory_space_constraint(value, pltpu.HBM)

    total, halves = pl.pallas_call(
        functools.partial(kernel, sizes),
        out_shape=(
            jax.ShapeDtypeStruct((tok, wide), F32),
            jax.ShapeDtypeStruct((2, half_hid, width), F32),
        ),
        in_specs=[hbm] * 7,
        out_specs=(vmem, vmem),
        scratch_shapes=[
            pltpu.VMEM((tok, LANES), BF16),
            pltpu.VMEM((nz, tok, wide), BF16),
            pltpu.VMEM((nz, tok, width), BF16),
            pltpu.VMEM((batches, 4 * tok, count), BF16),
            pltpu.VMEM((nz // 2, ny, block, width), BF16),
            pltpu.VMEM((nz // 2, ny, block, width), BF16),
            pltpu.VMEM((3, nx, 2, half_hid, width), BF16),
            pltpu.VMEM((batches, 2 * count, hidden), BF16),
            pltpu.VMEM((count, hidden), BF16),
            pltpu.VMEM((count, hidden), BF16),
            pltpu.VMEM((batches, ny, block, wide), BF16),
            pltpu.VMEM((batches, ny, block, wide), BF16),
            pltpu.VMEM((nz, tok, wide), F32),
            pltpu.VMEM((half + 1, tok, wide), BF16),
            pltpu.VMEM((half, tok, wide), BF16),
            pltpu.VMEM((half + 1, tok, wide), BF16),
            pltpu.VMEM((half, tok, wide), BF16),
            pltpu.VMEM((nx, 2, half_hid, width), F32),
            pltpu.VMEM((nx, half_hid, width), BF16),
            pltpu.VMEM((nx, half_hid, width), BF16),
            pltpu.VMEM((nx, half_hid, width), BF16),
            pltpu.VMEM((nx, half_hid, width), BF16),
            pltpu.VMEM((half_hid, width), F32),
            pltpu.VMEM((half_hid, width), F32),
            pltpu.VMEM((4, tok), jnp.int32),
            pltpu.VMEM((4, tok), BF16),
            pltpu.SemaphoreType.DMA((256,)),
            pltpu.SemaphoreType.DMA((256,)),
            pltpu.SemaphoreType.DMA((10,)),
        ],
        compiler_params=pltpu.CompilerParams(
            collective_id=0, has_side_effects=True, vmem_limit_bytes=48 << 20
        ),
    )(
        stay(tokens), stay(upstream), stay(ids), stay(scales),
        stay(gate_weight[0]), stay(up_weight[0]), stay(down_weight[0]),
    )
    d_tokens, d_probs, grad = pl.pallas_call(
        finish,
        out_shape=(
            jax.ShapeDtypeStruct((tok, width), BF16),
            jax.ShapeDtypeStruct((4, tok), BF16),
            jax.ShapeDtypeStruct((2, half_hid, width), F32),
        ),
        in_specs=[anywhere, anywhere, hbm, hbm],
        out_specs=(vmem, vmem, anywhere),
        scratch_shapes=[
            pltpu.VMEM((tok, wide), F32), pltpu.VMEM((4, tok), jnp.int32),
            pltpu.VMEM((4, tok), BF16), pltpu.SemaphoreType.DMA((4,)),
        ],
        compiler_params=pltpu.CompilerParams(vmem_limit_bytes=8 << 20),
    )(total, halves, stay(ids), stay(scales))
    return d_tokens, d_probs.T, grad.reshape(1, hid, width)


def build(mesh, ny):
    sizes = (mesh.shape["dp"], ny, mesh.shape["ep"] // ny)
    flat = P(("rep", "ep", "dp"), None)
    split = P("ep", "dp", None)
    return jax.shard_map(
        functools.partial(local, sizes),
        mesh=mesh,
        in_specs=(flat, flat, flat, flat, split, split, split),
        out_specs=(flat, flat, split),
        check_vma=False,
    )


def solution(mesh):
    return build(mesh, 4)
```

```python
import functools

import jax
import jax.numpy as jnp
from jax import lax
from jax.experimental import pallas as pl
from jax.experimental.pallas import tpu as pltpu
from jax.sharding import PartitionSpec as P

MESH = pl.DeviceIdType.MESH
F32, BF16 = jnp.float32, jnp.bfloat16
CAP = 4
LANES = 128
TILE = 512


def dot_t(left, right):
    return lax.dot_general(left, right, (((1,), (1,)), ((), ())), preferred_element_type=F32)


def dot_n(left, right):
    return lax.dot_general(left, right, (((1,), (0,)), ((), ())), preferred_element_type=F32)


def tiles(width):
    return [(start, min(TILE, width - start)) for start in range(0, width, TILE)]


def kernel(
    sizes, tok_ref, ups_ref, ids_ref, rw_ref, gate_ref, up_ref, down_ref,
    total_ref, grad_ref,
    meta, xa, dya, seltr, stage, rows, weights, act, dgate, dup, dxs, ret, part,
    fsend, frecv, bsend, brecv, gacc, gsend, gpart, ssend, srecv, gfin, gother,
    ids_own, rw_own, spsend, sprecv, lbuf, spread_in, dxq, dxe, pack7, pack8,
    rsend7, rsend8, rrecv7, rrecv8, take7, take8, send_sem, recv_sem, local_sem,
):
    nx, ny, nz = sizes
    tok, width = tok_ref.shape
    hid = gate_ref.shape[0]
    half_hid = hid // 2
    hidden = nx * hid
    near = nz // 2 - 2
    batches = nz // 4
    last = batches - 1
    own = 2 * near
    wide = width + LANES
    quarter = width // 4
    core, ep, dp = lax.axis_index("rep"), lax.axis_index("ep"), lax.axis_index("dp")
    z, y = ep // ny, lax.rem(ep, ny)

    def at_z(step):
        return (core, lax.rem(z + step + nz, nz) * ny + y, dp)

    def at_y(step):
        return (core, z * ny + lax.rem(y + step, ny), dp)

    def at_x(step):
        return (core, ep, lax.rem(dp + step, nx))

    partner = (1 - core, ep, dp)

    def at_zy(step, side):
        return (core, lax.rem(z + step + nz, nz) * ny + lax.rem(y + side, ny), dp)

    order = []
    for step in range(1, near + 1):
        order += [-step, step]
    place = {delta: index for index, delta in enumerate(order + [0])}

    started = []

    def send(src, dst, device):
        index = len(started)
        copy = pltpu.make_async_remote_copy(
            src_ref=src, dst_ref=dst, send_sem=send_sem.at[index],
            recv_sem=recv_sem.at[index], device_id=device, device_id_type=MESH,
        )
        copy.start()
        started.append(copy)
        return copy

    shard_refs = (gate_ref, up_ref, down_ref)
    mine = pl.ds(pl.multiple_of(core * half_hid, half_hid), half_hid)
    theirs = pl.ds(pl.multiple_of((1 - core) * half_hid, half_hid), half_hid)
    loads = [(ids_ref, ids_own), (rw_ref, rw_own), (tok_ref, xa.at[own, :, pl.ds(0, width)]), (ups_ref, dya.at[own])]
    for index, ref in enumerate(shard_refs):
        loads.append((ref.at[mine], weights.at[index, 0, 0]))
        loads.append((ref.at[theirs], weights.at[index, 0, 1]))
    loads = [
        pltpu.make_async_copy(src, dst, local_sem.at[index])
        for index, (src, dst) in enumerate(loads)
    ]
    for copy in loads:
        copy.start()

    barrier = pltpu.get_barrier_semaphore()
    peers = [at_zy(step, side) for step in (-2, -1, 1, 2) for side in range(ny)] + [partner]
    peers += [at_y(step) for step in range(1, ny)]
    peers += [at_x(step) for step in range(1, nx)]
    for peer in peers:
        pl.semaphore_signal(barrier, inc=1, device_id=peer, device_id_type=MESH)
    loads[0].wait()
    loads[1].wait()
    pl.semaphore_wait(barrier, len(peers))

    xcopy, dcopy, mcopy = {}, {}, {}

    def first_x(sign):
        xcopy[sign] = send(tok_ref, xa.at[place[sign], :, pl.ds(0, width)], at_z(-sign))

    def first_d(sign):
        dcopy[sign] = send(ups_ref, dya.at[place[sign]], at_z(-sign))

    def first_m(sign):
        mcopy[sign] = send(meta, xa.at[place[sign], :, pl.ds(width, LANES)], at_z(-sign))

    first_x(-1)
    first_d(1)

    name = lax.broadcasted_iota(jnp.int32, (LANES, tok), 0)
    scales = rw_own[...].astype(F32)
    routed = jnp.zeros((LANES, tok), F32)
    scale = jnp.zeros((LANES, tok), F32)
    for k in range(4):
        chosen_name = ids_own[k:k + 1, :]
        routed = routed + jnp.where(name == chosen_name, 1.0, 0.0)
        scale = scale + jnp.where(name == chosen_name + 64, scales[k:k + 1, :], 0.0)
    first = lax.broadcasted_iota(jnp.int32, (tok, tok), 0)
    second = lax.broadcasted_iota(jnp.int32, (tok, tok), 1)
    upper = jnp.where(first < second, 1.0, 0.0).astype(BF16)
    same = jnp.where(first == second, 1.0, 0.0).astype(BF16)
    rank = routed * (dot_n(routed.astype(BF16), upper) + 1.0)
    own_meta = dot_t(same, (rank + scale).astype(BF16)).astype(BF16)
    meta[...] = own_meta
    first_m(-1)
    first_x(1)
    first_m(1)
    first_d(-1)
    xa[own, :, width:wide] = own_meta

    wcopy = {}
    for index, ref in enumerate(shard_refs):
        wcopy[index, nx - 1] = send(ref.at[mine], weights.at[index, nx - 1, 0], at_x(1))
        if nx == 4:
            wcopy[index, 1] = send(ref.at[mine], weights.at[index, 1, 0], at_x(3))
    for copy in loads[2:]:
        copy.wait()

    hcopy = []

    def near_weights():
        for index in range(3):
            wcopy[index, nx - 1].wait_recv()
            if nx == 4:
                wcopy[index, 1].wait_recv()
                if index == 1:
                    wcopy[index, 2] = send(weights.at[index, 1, 0], weights.at[index, 2, 0], at_x(3))
                else:
                    wcopy[index, 2] = send(weights.at[index, 3, 0], weights.at[index, 2, 0], at_x(1))
        for index in range(3):
            for rel in ((1, 3) if nx == 4 else (1,)):
                hcopy.append(send(weights.at[index, rel, 0], weights.at[index, rel, 1], partner))

    def far_weights():
        if nx == 4:
            for index in range(3):
                wcopy[index, 2].wait_recv()
                hcopy.append(send(weights.at[index, 2, 0], weights.at[index, 2, 1], partner))

    def all_weights():
        for copy in hcopy:
            copy.wait_recv()

    ycopy = {}
    block = 2 * CAP
    count = ny * block

    def chosen(value, r, c, sources):
        slot = (lax.rem(r, CAP) + 1).astype(F32)
        return (value == slot) & (c // tok == lax.rem(r // CAP, sources))

    def picks(size, row_block, plane=0):
        row = lax.broadcasted_iota(jnp.int32, (size, LANES), 0)
        col = lax.broadcasted_iota(jnp.int32, (size, LANES), 1)
        expert = lax.rem(z + plane + nz, nz) * ny + lax.rem(y + row // row_block, ny)
        pick = jnp.where(col == expert, 1.0, 0.0).astype(BF16)
        pick_w = jnp.where(col == expert + 64, 1.0, 0.0).astype(BF16)
        return pick, pick_w

    def dispatch(p):
        low, high = (2 * p, 2 * p + 2) if p < near else (own, own + 1)
        size_t = (high - low) * tok
        group = xa[low:high, :, width:wide].reshape(size_t, LANES)
        pick, pick_w = picks(count, block)
        shape = (count, size_t)
        r, c = (lax.broadcasted_iota(jnp.int32, shape, axis) for axis in (0, 1))
        hit = chosen(dot_t(pick, group), r, c, 2)
        sel = jnp.where(hit, 1.0, 0.0).astype(BF16)
        sel_w = jnp.where(hit, dot_t(pick_w, group), 0.0).astype(BF16)
        for start, size in tiles(width):
            parts = []
            for source, chooser in ((xa, sel), (dya, sel_w)):
                value = source[low:high, :, start:start + size].reshape(size_t, size)
                parts.append(dot_n(chooser, value).reshape(ny, block, size))
            out = jnp.concatenate(parts, axis=1).astype(BF16)
            rows[p, 0, :, start:start + size] = out[0]
            stage[p, 1:ny, :, start:start + size] = out[1:ny]
        for step in range(1, ny):
            ycopy[p, step] = send(stage.at[p, step], rows.at[p, ny - step], at_y(step))

    spcopy = []

    def special(sign, kind, planes):
        source = (xa, dya)[kind]
        index = place[sign * near]
        group = xa[index, :, width:wide]
        group = jnp.concatenate([group] * 4, axis=0)
        value = jnp.concatenate(
            [source[index, :, quarter * q:quarter * (q + 1)] for q in range(4)], axis=0
        )
        for plane in planes:
            pick, pick_w = picks(2 * count, 2 * block, plane)
            shape = (2 * count, 4 * tok)
            r, c = (lax.broadcasted_iota(jnp.int32, shape, axis) for axis in (0, 1))
            hit = chosen(dot_t(pick, group), r, c, 4)
            sel = jnp.where(hit, dot_t(pick_w, group) if kind else 1.0, 0.0).astype(BF16)
            slot = {1: 0, -1: 1}.get(plane, 2)
            spsend[slot, kind] = dot_n(sel, value).astype(BF16).reshape(ny, 2 * block, quarter)
            for side in range(ny):
                spcopy.append(send(
                    spsend.at[slot, kind, side], sprecv.at[slot, kind, (ny - side) % ny], at_zy(plane, side)
                ))

    def digits(shape, axis, *sizes):
        value = lax.broadcasted_iota(jnp.int32, shape, axis)
        found = []
        for size in reversed(sizes):
            found.append(lax.rem(value, size))
            value = value // size
        return found[::-1]

    def constants():
        shape = (4 * count, 6 * 2 * count)
        rb, ry, rk, rj, rs = digits(shape, 0, 2, ny, 2, 2, CAP)
        ci, ck, cy, cq, cs = digits(shape, 1, 3, 2, ny, 4, CAP)
        wanted = jnp.where(rb == 1, rj, 3 * rj - 1)
        match = (ci == wanted) & (ck == rk) & (cy == ry) & (cs == rs)
        for q in range(4):
            spread_in[q] = jnp.where(match & (cq == q), 1.0, 0.0).astype(BF16)

    def more_constants():
        shape = (4 * count, 8 * count)
        ri, ry, rq, rs = digits(shape, 0, 2, ny, 4, CAP)
        cq, cb, cy, cj, cs = digits(shape, 1, 4, 2, ny, 2, CAP)
        match = (cb == 1) & (cj == ri) & (cq == rq) & (cy == ry) & (cs == rs)
        pack7[...] = jnp.where(match, 1.0, 0.0).astype(BF16)
        shape = (2 * count, 8 * count)
        ri, ry, rq, rs = digits(shape, 0, 2, ny, 2, CAP)
        cq, cb, cy, cj, cs = digits(shape, 1, 4, 2, ny, 2, CAP)
        match = (cb == 0) & (cj == 1) & (cq == 2 * rq + ri) & (cy == ry) & (cs == rs)
        pack8[...] = jnp.where(match, 1.0, 0.0).astype(BF16)

    def takes():
        for side, sign in ((0, 1), (1, -1)):
            group = xa[place[sign * near], :, width:wide]
            pick, _ = picks(2 * count, 2 * block, -sign)
            shape = (tok, 2 * count)
            _, cq, cs = digits(shape, 1, ny, 4, CAP)
            hit = dot_t(group, pick) == (cs + 1).astype(F32)
            for q in range(4):
                take7[side, q] = jnp.where(hit & (cq == q), 1.0, 0.0).astype(BF16)
            pick, _ = picks(count, block, -2 * sign)
            shape = (tok, count)
            _, cq, cs = digits(shape, 1, ny, 2, CAP)
            hit = dot_t(group, pick) == (cs + 1).astype(F32)
            for q in range(2):
                take8[side, q] = jnp.where(hit & (cq == q), 1.0, 0.0).astype(BF16)

    def gather_last():
        for step in range(1, ny):
            ycopy[near, step].wait_recv()
        for copy in spcopy:
            copy.wait_recv()
        value = sprecv[...].reshape(12 * count, quarter)
        for q in range(4):
            out = dot_n(spread_in[q], value)
            base = rows[near, :, :, quarter * q:quarter * (q + 1)].reshape(2 * count, quarter).astype(F32)
            lbuf[0:2 * count, quarter * q:quarter * (q + 1)] = (out[0:2 * count] + base).astype(BF16)
            lbuf[2 * count:4 * count, quarter * q:quarter * (q + 1)] = out[2 * count:4 * count].astype(BF16)

    pcopy = []

    def give_far():
        value = dxq[...].reshape(8 * count, quarter)
        out7 = dot_n(pack7[...], value).astype(BF16).reshape(2, ny, 2 * block, quarter)
        out8 = dot_n(pack8[...], value).astype(BF16).reshape(2, ny, block, quarter)
        rsend7[:, :, :, 0:quarter] = out7
        rsend8[:, :, :, 0:quarter] = out8
        extra = dxe[...]
        extra = jnp.concatenate([jnp.zeros_like(extra)] * 3 + [extra], axis=0)
        rsend7[:, :, :, quarter:] = dot_n(pack7[...], extra).astype(BF16).reshape(2, ny, 2 * block, LANES)
        rsend8[:, :, :, quarter:] = dot_n(pack8[...], extra).astype(BF16).reshape(2, ny, block, LANES)
        for way, sign in ((0, 1), (1, -1)):
            for side in range(ny):
                there = (ny - side) % ny
                pcopy.append(send(rsend7.at[1 - way, side], rrecv7.at[way, there], at_zy(sign, side)))
                pcopy.append(send(rsend8.at[way, side], rrecv8.at[way, there], at_zy(2 * sign, side)))

    rcopy = {}
    edges = [(width // 4 * c, width // 4 if c < 3 else wide - width // 4 * 3) for c in range(4)]
    cols = [pl.ds(start, size) for start, size in edges]

    def split(value):
        value = value.reshape(2 * ny, 2, block, hidden)
        return value[:, 0], value[:, 1]

    def forward(b):
        if b < last:
            for p in (2 * b, 2 * b + 1):
                for step in range(1, ny):
                    ycopy[p, step].wait_recv()
            both = rows[2 * b:2 * b + 2].reshape(4 * count, width)
        else:
            both = lbuf[...]
        gate_pre, _ = split(dot_t(both, weights[0].reshape(hidden, width)))
        up_pre, _ = split(dot_t(both, weights[1].reshape(hidden, width)))
        _, d_act = split(dot_t(both, weights[2].reshape(hidden, width)))
        sig = jax.nn.sigmoid(gate_pre)
        silu = gate_pre * sig
        act_rows = (silu * up_pre).astype(BF16).astype(F32)
        act[b] = jnp.concatenate([jnp.zeros_like(act_rows), act_rows], axis=1).reshape(4 * count, hidden).astype(BF16)
        d_gate = d_act * up_pre * sig * (1.0 + gate_pre * (1.0 - sig))
        dgate[...] = d_gate.reshape(2 * count, hidden).astype(BF16)
        dup[...] = (d_act * silu).reshape(2 * count, hidden).astype(BF16)
        prob = jnp.sum(act_rows * d_act, axis=2, keepdims=True)
        here = lax.broadcasted_iota(jnp.int32, (2 * ny, block, LANES), 2) == ep
        give(b, width, LANES, jnp.where(here, prob, 0.0))

    def give(b, start, size, value):
        if b == last:
            if size == LANES:
                dxe[...] = value.reshape(2 * count, size).astype(BF16)
            else:
                dxq[start // quarter] = value.reshape(2 * count, size).astype(BF16)
        value = value.reshape(2, ny, block, size)
        value = jnp.concatenate([value[0], value[1]], axis=1).astype(BF16)
        dxs[b, 1:ny, :, start:start + size] = value[1:ny]
        ret[b, 0, :, start:start + size] = value[0]

    def backward(b):
        d_gate, d_up = dgate[...], dup[...]
        for col in range(4):
            start, size = quarter * col, quarter
            gate_t = weights[0, :, :, :, start:start + size].reshape(hidden, size)
            up_t = weights[1, :, :, :, start:start + size].reshape(hidden, size)
            give(b, start, size, dot_n(d_gate, gate_t) + dot_n(d_up, up_t))
        if b == last:
            give_far()
        for step in range(1, ny):
            rcopy[b, 0, step] = send(dxs.at[b, step], ret.at[b, ny - step], at_y(step))

    def spread(b):
        low, high = (4 * b, 4 * b + 4) if b < last else (own, own + 1)
        size_t = (high - low) * tok
        group = xa[low:high, :, width:wide].reshape(size_t, LANES)
        pick, _ = picks(2 * count, 2 * block)
        shape = (size_t, 2 * count)
        c, r = (lax.broadcasted_iota(jnp.int32, shape, axis) for axis in (0, 1))
        seltr[b, 0:size_t] = jnp.where(chosen(dot_t(group, pick), r, c, 4), 1.0, 0.0).astype(BF16)

    def combine(b, col):
        if (b, col, ny - 1) in rcopy:
            for step in range(1, ny):
                rcopy[b, col, step].wait_recv()
        start, size = edges[col]
        value = ret[b, :, :, start:start + size].reshape(2 * count, size)
        if b < last:
            part[4 * b:4 * b + 4, :, start:start + size] = dot_n(seltr[b], value).reshape(4, tok, size)
        else:
            part[own, :, start:start + size] = dot_n(seltr[b, 0:tok], value)

    def grads(b):
        act_t = act[b].T
        for start, size in tiles(width):
            if b < last:
                value = rows[2 * b:2 * b + 2, :, :, start:start + size].reshape(4 * count, size)
            else:
                value = lbuf[:, start:start + size]
            out = dot_n(act_t, value).reshape(nx, 2, half_hid, size)
            if b:
                out = out + gacc[:, :, :, start:start + size]
            gacc[:, :, :, start:start + size] = out
            if b == batches - 1:
                gsend[:, :, start:start + size] = out[:, 1].astype(BF16)

    table = {
        2: [lambda: dispatch(near)], 4: [near_weights], 5: [constants], 7: [more_constants],
        8: [far_weights], 9: [all_weights, lambda: forward(0)],
        10: [lambda: backward(0)], 11: [lambda: forward(1)],
        12: [lambda: special(-1, 0, (2, 1)), lambda: backward(1)],
        13: [lambda: special(1, 1, (-2, -1)), lambda: special(1, 0, (-1,)), lambda: special(-1, 1, (1,))],
    }

    for step in range(1, near + 1):
        for slot, routes in (
            (2 * step, ((xa, xcopy, -1), (dya, dcopy, 1))),
            (2 * step + 1, ((dya, dcopy, -1), (xa, xcopy, 1))),
        ):
            for moving, copies, sign in routes:
                copies[sign * step].wait_recv()
                if step == 1 and moving is xa:
                    mcopy[sign].wait_recv()
                if step < near:
                    copies[sign * (step + 1)] = send(
                        moving.at[place[sign * step]], moving.at[place[sign * (step + 1)]], at_z(-sign)
                    )
            for task in table.get(slot, ()):
                task()
            if slot == 2 * step + 1:
                dispatch(step - 1)

    takes()
    grads(0)
    grads(1)
    spread(0)
    spread(1)
    forward(2)
    backward(2)
    gather_last()
    forward(last)
    backward(last)
    for b in range(2, batches):
        grads(b)
    gcopy = send(gsend, gpart, partner)
    for b in range(batches):
        if b > 1:
            spread(b)
        if b < last:
            for col in range(4):
                combine(b, col)

    def pair_sum():
        gcopy.wait_recv()
        for rel in range(nx):
            total = gacc[rel, 0] + gpart[rel].astype(F32)
            if rel:
                ssend[rel] = total.astype(BF16)
            else:
                gacc[0, 0] = total
        return [send(ssend.at[rel], srecv.at[nx - rel], at_x(rel)) for rel in range(1, nx)]

    chain = {}

    def relay(col, sign, dist):
        sends, recvs = (fsend, frecv) if sign == 1 else (bsend, brecv)
        value = part[place[sign * dist], :, cols[col]]
        if dist == near:
            way, size = (1 - sign) // 2, edges[col][1]
            far = rrecv7[way, :, :, 0:size].reshape(2 * count, size)
            value = value + dot_n(take7[way, col], far)
            if col % 2 == way:
                far = rrecv8[way, :, :, 0:size].reshape(count, size)
                value = value + dot_n(take8[way, col // 2], far)
        else:
            chain[col, sign, dist].wait_recv()
            value = value + recvs[dist, :, cols[col]].astype(F32)
        sends[dist, :, cols[col]] = value.astype(BF16)
        chain[col, sign, dist - 1] = send(
            sends.at[dist, :, cols[col]], recvs.at[dist - 1, :, cols[col]], at_z(sign)
        )

    for copy in pcopy:
        copy.wait_recv()
    for turn in range(near):
        for col in range(4):
            relay(col, 1, near - turn)
            relay(col, -1, near - turn)
        if turn == 0:
            scopy = pair_sum()
            for col in range(4):
                combine(last, col)
        if turn == near - 2:
            total = gacc[0, 0]
            for rel in range(1, nx):
                scopy[rel - 1].wait_recv()
            for rel in range(1, nx):
                total = total + srecv[rel].astype(F32)
            gfin[...] = total
            grad_ref[core] = total
            fin = send(gfin, gother, partner)
    fin.wait_recv()
    grad_ref[1 - core] = gother[...]
    for col in range(4):
        chain[col, 1, 0].wait_recv()
        chain[col, -1, 0].wait_recv()
        start, size = edges[col]
        total_ref[:, start:start + size] = (
            part[own, :, start:start + size]
            + frecv[0, :, start:start + size].astype(F32)
            + brecv[0, :, start:start + size].astype(F32)
        )
    for copy in started:
        copy.wait_send()


def finish(total_any, halves_ref, ids_any, rw_any, dtok_ref, dprob_ref, grad_ref, total_ref, ids_ref, rw_ref, sem):
    tok, width = dtok_ref.shape
    grad_copy = pltpu.make_async_copy(halves_ref, grad_ref, sem.at[0])
    total_copy = pltpu.make_async_copy(total_any, total_ref, sem.at[1])
    ids_copy = pltpu.make_async_copy(ids_any, ids_ref, sem.at[2])
    rw_copy = pltpu.make_async_copy(rw_any, rw_ref, sem.at[3])
    for copy in (ids_copy, rw_copy, total_copy, grad_copy):
        copy.start()
    total_copy.wait()
    dtok_ref[...] = total_ref[:, 0:width].astype(BF16)
    probs = total_ref[:, width:width + LANES].astype(BF16)
    name = lax.broadcasted_iota(jnp.int32, (LANES, LANES), 0)
    other = lax.broadcasted_iota(jnp.int32, (LANES, LANES), 1)
    same = jnp.where(name == other, 1.0, 0.0).astype(BF16)
    probs = dot_t(same, probs)
    ids_copy.wait()
    rw_copy.wait()
    name = lax.broadcasted_iota(jnp.int32, (LANES, tok), 0)
    slot = lax.broadcasted_iota(jnp.int32, (4, tok), 0)
    values = jnp.zeros((4, tok), F32)
    for k in range(4):
        value = jnp.sum(jnp.where(name == ids_ref[k:k + 1, :], probs, 0.0), axis=0, keepdims=True)
        values = jnp.where(slot == k, value, values)
    dprob_ref[...] = (values / rw_ref[...].astype(F32)).astype(BF16)
    grad_copy.wait()


def local(sizes, tokens, upstream, expert_ids, route_weight, gate_weight, up_weight, down_weight):
    nx, ny, nz = sizes
    tok, width = tokens.shape
    hid = gate_weight.shape[1]
    half_hid, hidden = hid // 2, hid * nx
    half, batches = nz // 2, nz // 4
    wide, block, quarter = width + LANES, 4 * CAP, width // 4
    count = ny * block
    vmem = pl.BlockSpec(memory_space=pltpu.VMEM)
    hbm = pl.BlockSpec(memory_space=pltpu.HBM)
    anywhere = pl.BlockSpec(memory_space=pl.ANY)
    ids, scales = expert_ids.T, route_weight.T

    def stay(value):
        return pltpu.with_memory_space_constraint(value, pltpu.HBM)

    total, halves = pl.pallas_call(
        functools.partial(kernel, sizes),
        out_shape=(
            jax.ShapeDtypeStruct((tok, wide), F32),
            jax.ShapeDtypeStruct((2, half_hid, width), F32),
        ),
        in_specs=[hbm] * 7,
        out_specs=(vmem, vmem),
        scratch_shapes=[
            pltpu.VMEM((tok, LANES), BF16),
            pltpu.VMEM((nz, tok, wide), BF16),
            pltpu.VMEM((nz, tok, width), BF16),
            pltpu.VMEM((batches, 4 * tok, count), BF16),
            pltpu.VMEM((nz // 2, ny, block, width), BF16),
            pltpu.VMEM((nz // 2, ny, block, width), BF16),
            pltpu.VMEM((3, nx, 2, half_hid, width), BF16),
            pltpu.VMEM((batches, 2 * count, hidden), BF16),
            pltpu.VMEM((count, hidden), BF16),
            pltpu.VMEM((count, hidden), BF16),
            pltpu.VMEM((batches, ny, block, wide), BF16),
            pltpu.VMEM((batches, ny, block, wide), BF16),
            pltpu.VMEM((nz, tok, wide), F32),
            pltpu.VMEM((half + 1, tok, wide), BF16),
            pltpu.VMEM((half, tok, wide), BF16),
            pltpu.VMEM((half + 1, tok, wide), BF16),
            pltpu.VMEM((half, tok, wide), BF16),
            pltpu.VMEM((nx, 2, half_hid, width), F32),
            pltpu.VMEM((nx, half_hid, width), BF16),
            pltpu.VMEM((nx, half_hid, width), BF16),
            pltpu.VMEM((nx, half_hid, width), BF16),
            pltpu.VMEM((nx, half_hid, width), BF16),
            pltpu.VMEM((half_hid, width), F32),
            pltpu.VMEM((half_hid, width), F32),
            pltpu.VMEM((4, tok), jnp.int32),
            pltpu.VMEM((4, tok), BF16),
            pltpu.VMEM((3, 2, ny, block, quarter), BF16),
            pltpu.VMEM((3, 2, ny, block, quarter), BF16),
            pltpu.VMEM((2 * count, width), BF16),
            pltpu.VMEM((4, 2 * count, 6 * count), BF16),
            pltpu.VMEM((4, count, quarter), BF16),
            pltpu.VMEM((count, LANES), BF16),
            pltpu.VMEM((2 * count, 4 * count), BF16),
            pltpu.VMEM((count, 4 * count), BF16),
            pltpu.VMEM((2, ny, block, quarter + LANES), BF16),
            pltpu.VMEM((2, ny, block // 2, quarter + LANES), BF16),
            pltpu.VMEM((2, ny, block, quarter + LANES), BF16),
            pltpu.VMEM((2, ny, block // 2, quarter + LANES), BF16),
            pltpu.VMEM((2, 4, tok, count), BF16),
            pltpu.VMEM((2, 2, tok, count // 2), BF16),
            pltpu.SemaphoreType.DMA((256,)),
            pltpu.SemaphoreType.DMA((256,)),
            pltpu.SemaphoreType.DMA((10,)),
        ],
        compiler_params=pltpu.CompilerParams(
            collective_id=0, has_side_effects=True, vmem_limit_bytes=48 << 20
        ),
    )(
        stay(tokens), stay(upstream), stay(ids), stay(scales),
        stay(gate_weight[0]), stay(up_weight[0]), stay(down_weight[0]),
    )
    d_tokens, d_probs, grad = pl.pallas_call(
        finish,
        out_shape=(
            jax.ShapeDtypeStruct((tok, width), BF16),
            jax.ShapeDtypeStruct((4, tok), BF16),
            jax.ShapeDtypeStruct((2, half_hid, width), F32),
        ),
        in_specs=[anywhere, anywhere, hbm, hbm],
        out_specs=(vmem, vmem, anywhere),
        scratch_shapes=[
            pltpu.VMEM((tok, wide), F32), pltpu.VMEM((4, tok), jnp.int32),
            pltpu.VMEM((4, tok), BF16), pltpu.SemaphoreType.DMA((4,)),
        ],
        compiler_params=pltpu.CompilerParams(vmem_limit_bytes=8 << 20),
    )(total, halves, stay(ids), stay(scales))
    return d_tokens, d_probs.T, grad.reshape(1, hid, width)


def build(mesh, ny):
    sizes = (mesh.shape["dp"], ny, mesh.shape["ep"] // ny)
    flat = P(("rep", "ep", "dp"), None)
    split = P("ep", "dp", None)
    return jax.shard_map(
        functools.partial(local, sizes),
        mesh=mesh,
        in_specs=(flat, flat, flat, flat, split, split, split),
        out_specs=(flat, flat, split),
        check_vma=False,
    )


def solution(mesh):
    return build(mesh, 4)
```

```python
import functools

import jax
import jax.numpy as jnp
from jax import lax
from jax.experimental import pallas as pl
from jax.experimental.pallas import tpu as pltpu
from jax.sharding import PartitionSpec as P

MESH = pl.DeviceIdType.MESH
F32, BF16 = jnp.float32, jnp.bfloat16
CAP = 4
LANES = 128
TILE = 512


def dot_t(left, right):
    return lax.dot_general(left, right, (((1,), (1,)), ((), ())), preferred_element_type=F32)


def dot_n(left, right):
    return lax.dot_general(left, right, (((1,), (0,)), ((), ())), preferred_element_type=F32)


def tiles(width):
    return [(start, min(TILE, width - start)) for start in range(0, width, TILE)]


def kernel(
    sizes, tok_ref, ups_ref, ids_ref, rw_ref, gate_ref, up_ref, down_ref,
    total_ref, grad_ref,
    meta, xa, dya, seltr, stage, rows, weights, act, dgate, dup, dxs, ret, part,
    fsend, frecv, bsend, brecv, gacc, gsend, gpart, ssend, srecv, gfin, gother,
    ids_own, rw_own, spsend, sprecv, lbuf, spread_in, dxq, dxe, pack7, pack8,
    rsend7, rsend8, rrecv7, rrecv8, take7, take8, send_sem, recv_sem, local_sem,
):
    nx, ny, nz = sizes
    tok, width = tok_ref.shape
    hid = gate_ref.shape[0]
    half_hid = hid // 2
    hidden = nx * hid
    near = nz // 2 - 2
    batches = nz // 4
    last = batches - 1
    own = 2 * near
    wide = width + LANES
    quarter = width // 4
    core, ep, dp = lax.axis_index("rep"), lax.axis_index("ep"), lax.axis_index("dp")
    z, y = ep // ny, lax.rem(ep, ny)

    def at_z(step):
        return (core, lax.rem(z + step + nz, nz) * ny + y, dp)

    def at_y(step):
        return (core, z * ny + lax.rem(y + step, ny), dp)

    def at_x(step):
        return (core, ep, lax.rem(dp + step, nx))

    partner = (1 - core, ep, dp)

    def at_zy(step, side):
        return (core, lax.rem(z + step + nz, nz) * ny + lax.rem(y + side, ny), dp)

    order = []
    for step in range(1, near + 1):
        order += [-step, step]
    place = {delta: index for index, delta in enumerate(order + [0])}

    started = []

    def send(src, dst, device):
        index = len(started)
        copy = pltpu.make_async_remote_copy(
            src_ref=src, dst_ref=dst, send_sem=send_sem.at[index],
            recv_sem=recv_sem.at[index], device_id=device, device_id_type=MESH,
        )
        copy.start()
        started.append(copy)
        return copy

    shard_refs = (gate_ref, up_ref, down_ref)
    mine = pl.ds(pl.multiple_of(core * half_hid, half_hid), half_hid)
    theirs = pl.ds(pl.multiple_of((1 - core) * half_hid, half_hid), half_hid)
    loads = [(ids_ref, ids_own), (rw_ref, rw_own), (tok_ref, xa.at[own, :, pl.ds(0, width)]), (ups_ref, dya.at[own])]
    for index, ref in enumerate(shard_refs):
        loads.append((ref.at[mine], weights.at[index, 0, 0]))
        loads.append((ref.at[theirs], weights.at[index, 0, 1]))
    loads = [
        pltpu.make_async_copy(src, dst, local_sem.at[index])
        for index, (src, dst) in enumerate(loads)
    ]
    for copy in loads:
        copy.start()

    barrier = pltpu.get_barrier_semaphore()
    peers = [at_zy(step, side) for step in (-2, -1, 1, 2) for side in range(ny)] + [partner]
    peers += [at_y(step) for step in range(1, ny)]
    peers += [at_x(step) for step in range(1, nx)]
    for peer in peers:
        pl.semaphore_signal(barrier, inc=1, device_id=peer, device_id_type=MESH)
    loads[0].wait()
    loads[1].wait()
    pl.semaphore_wait(barrier, len(peers))

    xcopy, dcopy, mcopy = {}, {}, {}

    def first_x(sign):
        xcopy[sign] = send(tok_ref, xa.at[place[sign], :, pl.ds(0, width)], at_z(-sign))

    def first_d(sign):
        dcopy[sign] = send(ups_ref, dya.at[place[sign]], at_z(-sign))

    def first_m(sign):
        mcopy[sign] = send(meta, xa.at[place[sign], :, pl.ds(width, LANES)], at_z(-sign))

    first_x(-1)
    first_d(1)

    name = lax.broadcasted_iota(jnp.int32, (LANES, tok), 0)
    scales = rw_own[...].astype(F32)
    routed = jnp.zeros((LANES, tok), F32)
    scale = jnp.zeros((LANES, tok), F32)
    for k in range(4):
        chosen_name = ids_own[k:k + 1, :]
        routed = routed + jnp.where(name == chosen_name, 1.0, 0.0)
        scale = scale + jnp.where(name == chosen_name + 64, scales[k:k + 1, :], 0.0)
    first = lax.broadcasted_iota(jnp.int32, (tok, tok), 0)
    second = lax.broadcasted_iota(jnp.int32, (tok, tok), 1)
    upper = jnp.where(first < second, 1.0, 0.0).astype(BF16)
    same = jnp.where(first == second, 1.0, 0.0).astype(BF16)
    rank = routed * (dot_n(routed.astype(BF16), upper) + 1.0)
    own_meta = dot_t(same, (rank + scale).astype(BF16)).astype(BF16)
    meta[...] = own_meta
    first_m(-1)
    first_x(1)
    first_m(1)
    first_d(-1)
    xa[own, :, width:wide] = own_meta

    wcopy = {}
    for index, ref in enumerate(shard_refs):
        wcopy[index, nx - 1] = send(ref.at[mine], weights.at[index, nx - 1, 0], at_x(1))
        if nx == 4:
            wcopy[index, 1] = send(ref.at[mine], weights.at[index, 1, 0], at_x(3))
    for copy in loads[2:]:
        copy.wait()

    hcopy = []

    def near_weights():
        for index in range(3):
            wcopy[index, nx - 1].wait_recv()
            if nx == 4:
                wcopy[index, 1].wait_recv()
                if index == 1:
                    wcopy[index, 2] = send(weights.at[index, 1, 0], weights.at[index, 2, 0], at_x(3))
                else:
                    wcopy[index, 2] = send(weights.at[index, 3, 0], weights.at[index, 2, 0], at_x(1))
        for index in range(3):
            for rel in ((1, 3) if nx == 4 else (1,)):
                hcopy.append(send(weights.at[index, rel, 0], weights.at[index, rel, 1], partner))

    def far_weights():
        if nx == 4:
            for index in range(3):
                wcopy[index, 2].wait_recv()
                hcopy.append(send(weights.at[index, 2, 0], weights.at[index, 2, 1], partner))

    def all_weights():
        for copy in hcopy:
            copy.wait_recv()

    ycopy = {}
    block = 2 * CAP
    count = ny * block

    def chosen(value, r, c, sources):
        slot = (lax.rem(r, CAP) + 1).astype(F32)
        return (value == slot) & (c // tok == lax.rem(r // CAP, sources))

    def picks(size, row_block, plane=0):
        row = lax.broadcasted_iota(jnp.int32, (size, LANES), 0)
        col = lax.broadcasted_iota(jnp.int32, (size, LANES), 1)
        expert = lax.rem(z + plane + nz, nz) * ny + lax.rem(y + row // row_block, ny)
        pick = jnp.where(col == expert, 1.0, 0.0).astype(BF16)
        pick_w = jnp.where(col == expert + 64, 1.0, 0.0).astype(BF16)
        return pick, pick_w

    def dispatch(p):
        low, high = (2 * p, 2 * p + 2) if p < near else (own, own + 1)
        size_t = (high - low) * tok
        group = xa[low:high, :, width:wide].reshape(size_t, LANES)
        pick, pick_w = picks(count, block)
        shape = (count, size_t)
        r, c = (lax.broadcasted_iota(jnp.int32, shape, axis) for axis in (0, 1))
        hit = chosen(dot_t(pick, group), r, c, 2)
        sel = jnp.where(hit, 1.0, 0.0).astype(BF16)
        sel_w = jnp.where(hit, dot_t(pick_w, group), 0.0).astype(BF16)
        for start, size in tiles(width):
            parts = []
            for source, chooser in ((xa, sel), (dya, sel_w)):
                value = source[low:high, :, start:start + size].reshape(size_t, size)
                parts.append(dot_n(chooser, value).reshape(ny, block, size))
            out = jnp.concatenate(parts, axis=1).astype(BF16)
            rows[p, 0, :, start:start + size] = out[0]
            stage[p, 1:ny, :, start:start + size] = out[1:ny]
        for step in range(1, ny):
            ycopy[p, step] = send(stage.at[p, step], rows.at[p, ny - step], at_y(step))

    spcopy = []

    def special(sign, kind, planes):
        source = (xa, dya)[kind]
        index = place[sign * near]
        group = xa[index, :, width:wide]
        group = jnp.concatenate([group] * 4, axis=0)
        value = jnp.concatenate(
            [source[index, :, quarter * q:quarter * (q + 1)] for q in range(4)], axis=0
        )
        for plane in planes:
            pick, pick_w = picks(2 * count, 2 * block, plane)
            shape = (2 * count, 4 * tok)
            r, c = (lax.broadcasted_iota(jnp.int32, shape, axis) for axis in (0, 1))
            hit = chosen(dot_t(pick, group), r, c, 4)
            sel = jnp.where(hit, dot_t(pick_w, group) if kind else 1.0, 0.0).astype(BF16)
            slot = {1: 0, -1: 1}.get(plane, 2)
            spsend[slot, kind] = dot_n(sel, value).astype(BF16).reshape(ny, 2 * block, quarter)
            for side in range(ny):
                spcopy.append(send(
                    spsend.at[slot, kind, side], sprecv.at[slot, kind, (ny - side) % ny], at_zy(plane, side)
                ))

    def digits(shape, axis, *sizes):
        value = lax.broadcasted_iota(jnp.int32, shape, axis)
        found = []
        for size in reversed(sizes):
            found.append(lax.rem(value, size))
            value = value // size
        return found[::-1]

    def constants():
        shape = (4 * count, 6 * 2 * count)
        rb, ry, rk, rj, rs = digits(shape, 0, 2, ny, 2, 2, CAP)
        ci, ck, cy, cq, cs = digits(shape, 1, 3, 2, ny, 4, CAP)
        wanted = jnp.where(rb == 1, rj, 3 * rj - 1)
        match = (ci == wanted) & (ck == rk) & (cy == ry) & (cs == rs)
        for q in range(4):
            spread_in[q] = jnp.where(match & (cq == q), 1.0, 0.0).astype(BF16)

    def more_constants():
        shape = (4 * count, 8 * count)
        ri, ry, rq, rs = digits(shape, 0, 2, ny, 4, CAP)
        cq, cb, cy, cj, cs = digits(shape, 1, 4, 2, ny, 2, CAP)
        match = (cb == 1) & (cj == ri) & (cq == rq) & (cy == ry) & (cs == rs)
        pack7[...] = jnp.where(match, 1.0, 0.0).astype(BF16)
        shape = (2 * count, 8 * count)
        ri, ry, rq, rs = digits(shape, 0, 2, ny, 2, CAP)
        cq, cb, cy, cj, cs = digits(shape, 1, 4, 2, ny, 2, CAP)
        match = (cb == 0) & (cj == 1) & (cq == 2 * rq + ri) & (cy == ry) & (cs == rs)
        pack8[...] = jnp.where(match, 1.0, 0.0).astype(BF16)

    def takes():
        for side, sign in ((0, 1), (1, -1)):
            group = xa[place[sign * near], :, width:wide]
            pick, _ = picks(2 * count, 2 * block, -sign)
            shape = (tok, 2 * count)
            _, cq, cs = digits(shape, 1, ny, 4, CAP)
            hit = dot_t(group, pick) == (cs + 1).astype(F32)
            for q in range(4):
                take7[side, q] = jnp.where(hit & (cq == q), 1.0, 0.0).astype(BF16)
            pick, _ = picks(count, block, -2 * sign)
            shape = (tok, count)
            _, cq, cs = digits(shape, 1, ny, 2, CAP)
            hit = dot_t(group, pick) == (cs + 1).astype(F32)
            for q in range(2):
                take8[side, q] = jnp.where(hit & (cq == q), 1.0, 0.0).astype(BF16)

    def gather_last():
        for step in range(1, ny):
            ycopy[near, step].wait_recv()
        for copy in spcopy:
            copy.wait_recv()
        value = sprecv[...].reshape(12 * count, quarter)
        for q in range(4):
            out = dot_n(spread_in[q], value)
            base = rows[near, :, :, quarter * q:quarter * (q + 1)].reshape(2 * count, quarter).astype(F32)
            lbuf[0:2 * count, quarter * q:quarter * (q + 1)] = (out[0:2 * count] + base).astype(BF16)
            lbuf[2 * count:4 * count, quarter * q:quarter * (q + 1)] = out[2 * count:4 * count].astype(BF16)

    pcopy = []

    def give_far():
        value = dxq[...].reshape(8 * count, quarter)
        out7 = dot_n(pack7[...], value).astype(BF16).reshape(2, ny, 2 * block, quarter)
        out8 = dot_n(pack8[...], value).astype(BF16).reshape(2, ny, block, quarter)
        rsend7[:, :, :, 0:quarter] = out7
        rsend8[:, :, :, 0:quarter] = out8
        extra = dxe[...]
        extra = jnp.concatenate([jnp.zeros_like(extra)] * 3 + [extra], axis=0)
        rsend7[:, :, :, quarter:] = dot_n(pack7[...], extra).astype(BF16).reshape(2, ny, 2 * block, LANES)
        rsend8[:, :, :, quarter:] = dot_n(pack8[...], extra).astype(BF16).reshape(2, ny, block, LANES)
        for way, sign in ((0, 1), (1, -1)):
            for side in range(ny):
                there = (ny - side) % ny
                pcopy.append(send(rsend7.at[1 - way, side], rrecv7.at[way, there], at_zy(sign, side)))
                pcopy.append(send(rsend8.at[way, side], rrecv8.at[way, there], at_zy(2 * sign, side)))

    rcopy = {}
    edges = [(width // 4 * c, width // 4 if c < 3 else wide - width // 4 * 3) for c in range(4)]
    cols = [pl.ds(start, size) for start, size in edges]

    def split(value):
        value = value.reshape(2 * ny, 2, block, hidden)
        return value[:, 0], value[:, 1]

    def forward(b):
        if b < last:
            for p in (2 * b, 2 * b + 1):
                for step in range(1, ny):
                    ycopy[p, step].wait_recv()
            both = rows[2 * b:2 * b + 2].reshape(4 * count, width)
        else:
            both = lbuf[...]
        gate_pre, _ = split(dot_t(both, weights[0].reshape(hidden, width)))
        up_pre, _ = split(dot_t(both, weights[1].reshape(hidden, width)))
        _, d_act = split(dot_t(both, weights[2].reshape(hidden, width)))
        sig = jax.nn.sigmoid(gate_pre)
        silu = gate_pre * sig
        act_rows = (silu * up_pre).astype(BF16).astype(F32)
        act[b] = jnp.concatenate([jnp.zeros_like(act_rows), act_rows], axis=1).reshape(4 * count, hidden).astype(BF16)
        d_gate = d_act * up_pre * sig * (1.0 + gate_pre * (1.0 - sig))
        dgate[...] = d_gate.reshape(2 * count, hidden).astype(BF16)
        dup[...] = (d_act * silu).reshape(2 * count, hidden).astype(BF16)
        prob = jnp.sum(act_rows * d_act, axis=2, keepdims=True)
        here = lax.broadcasted_iota(jnp.int32, (2 * ny, block, LANES), 2) == ep
        give(b, width, LANES, jnp.where(here, prob, 0.0))

    def give(b, start, size, value):
        if b == last:
            if size == LANES:
                dxe[...] = value.reshape(2 * count, size).astype(BF16)
            else:
                dxq[start // quarter] = value.reshape(2 * count, size).astype(BF16)
        value = value.reshape(2, ny, block, size)
        value = jnp.concatenate([value[0], value[1]], axis=1).astype(BF16)
        dxs[b, 1:ny, :, start:start + size] = value[1:ny]
        ret[b, 0, :, start:start + size] = value[0]

    def backward(b):
        d_gate, d_up = dgate[...], dup[...]
        for col in range(4):
            start, size = quarter * col, quarter
            gate_t = weights[0, :, :, :, start:start + size].reshape(hidden, size)
            up_t = weights[1, :, :, :, start:start + size].reshape(hidden, size)
            give(b, start, size, dot_n(d_gate, gate_t) + dot_n(d_up, up_t))
            if b == last - 1:
                for step in range(1, ny):
                    rcopy[b, col, step] = send(
                        dxs.at[b, step, :, cols[col]], ret.at[b, ny - step, :, cols[col]], at_y(step)
                    )
        if b == last:
            give_far()
        if b != last - 1:
            for step in range(1, ny):
                rcopy[b, 0, step] = send(dxs.at[b, step], ret.at[b, ny - step], at_y(step))

    def spread(b):
        low, high = (4 * b, 4 * b + 4) if b < last else (own, own + 1)
        size_t = (high - low) * tok
        group = xa[low:high, :, width:wide].reshape(size_t, LANES)
        pick, _ = picks(2 * count, 2 * block)
        shape = (size_t, 2 * count)
        c, r = (lax.broadcasted_iota(jnp.int32, shape, axis) for axis in (0, 1))
        seltr[b, 0:size_t] = jnp.where(chosen(dot_t(group, pick), r, c, 4), 1.0, 0.0).astype(BF16)

    def combine(b, col):
        if (b, col, ny - 1) in rcopy:
            for step in range(1, ny):
                rcopy[b, col, step].wait_recv()
        start, size = edges[col]
        value = ret[b, :, :, start:start + size].reshape(2 * count, size)
        if b < last:
            part[4 * b:4 * b + 4, :, start:start + size] = dot_n(seltr[b], value).reshape(4, tok, size)
        else:
            part[own, :, start:start + size] = dot_n(seltr[b, 0:tok], value)

    def grads(b):
        act_t = act[b].T
        for start, size in tiles(width):
            if b < last:
                value = rows[2 * b:2 * b + 2, :, :, start:start + size].reshape(4 * count, size)
            else:
                value = lbuf[:, start:start + size]
            out = dot_n(act_t, value).reshape(nx, 2, half_hid, size)
            if b:
                out = out + gacc[:, :, :, start:start + size]
            gacc[:, :, :, start:start + size] = out
            if b == batches - 1:
                gsend[:, :, start:start + size] = out[:, 1].astype(BF16)

    table = {
        2: [lambda: dispatch(near)], 4: [near_weights], 5: [constants], 7: [more_constants],
        8: [far_weights], 9: [all_weights, lambda: forward(0)],
        10: [lambda: backward(0)], 11: [lambda: forward(1)],
        12: [lambda: special(-1, 0, (2, 1)), lambda: backward(1)],
        13: [lambda: special(1, 1, (-2, -1)), lambda: special(1, 0, (-1,)), lambda: special(-1, 1, (1,))],
    }

    for step in range(1, near + 1):
        for slot, routes in (
            (2 * step, ((xa, xcopy, -1), (dya, dcopy, 1))),
            (2 * step + 1, ((dya, dcopy, -1), (xa, xcopy, 1))),
        ):
            for moving, copies, sign in routes:
                copies[sign * step].wait_recv()
                if step == 1 and moving is xa:
                    mcopy[sign].wait_recv()
                if step < near:
                    copies[sign * (step + 1)] = send(
                        moving.at[place[sign * step]], moving.at[place[sign * (step + 1)]], at_z(-sign)
                    )
            for task in table.get(slot, ()):
                task()
            if slot == 2 * step + 1:
                dispatch(step - 1)

    takes()
    grads(0)
    grads(1)
    spread(0)
    spread(1)
    spread(2)
    gather_last()
    forward(last)
    backward(last)
    forward(2)
    backward(2)
    for b in range(2, batches):
        grads(b)
    gcopy = send(gsend, gpart, partner)
    for b in range(batches):
        if b == last:
            spread(b)
        if b < last - 1:
            for col in range(4):
                combine(b, col)

    def pair_sum():
        gcopy.wait_recv()
        for rel in range(nx):
            total = gacc[rel, 0] + gpart[rel].astype(F32)
            if rel:
                ssend[rel] = total.astype(BF16)
            else:
                gacc[0, 0] = total
        return [send(ssend.at[rel], srecv.at[nx - rel], at_x(rel)) for rel in range(1, nx)]

    chain = {}

    def relay(col, sign, dist):
        sends, recvs = (fsend, frecv) if sign == 1 else (bsend, brecv)
        value = part[place[sign * dist], :, cols[col]]
        if dist == near:
            way, size = (1 - sign) // 2, edges[col][1]
            far = rrecv7[way, :, :, 0:size].reshape(2 * count, size)
            value = value + dot_n(take7[way, col], far)
            if col % 2 == way:
                far = rrecv8[way, :, :, 0:size].reshape(count, size)
                value = value + dot_n(take8[way, col // 2], far)
        else:
            chain[col, sign, dist].wait_recv()
            value = value + recvs[dist, :, cols[col]].astype(F32)
        sends[dist, :, cols[col]] = value.astype(BF16)
        chain[col, sign, dist - 1] = send(
            sends.at[dist, :, cols[col]], recvs.at[dist - 1, :, cols[col]], at_z(sign)
        )

    for copy in pcopy:
        copy.wait_recv()
    for turn in range(near):
        for col in range(4):
            if turn == 0:
                combine(last - 1, col)
            relay(col, 1, near - turn)
            relay(col, -1, near - turn)
        if turn == 0:
            scopy = pair_sum()
            for col in range(4):
                combine(last, col)
        if turn == near - 2:
            total = gacc[0, 0]
            for rel in range(1, nx):
                scopy[rel - 1].wait_recv()
            for rel in range(1, nx):
                total = total + srecv[rel].astype(F32)
            gfin[...] = total
            grad_ref[core] = total
            fin = send(gfin, gother, partner)
    fin.wait_recv()
    grad_ref[1 - core] = gother[...]
    for col in range(4):
        chain[col, 1, 0].wait_recv()
        chain[col, -1, 0].wait_recv()
        start, size = edges[col]
        total_ref[:, start:start + size] = (
            part[own, :, start:start + size]
            + frecv[0, :, start:start + size].astype(F32)
            + brecv[0, :, start:start + size].astype(F32)
        )
    for copy in started:
        copy.wait_send()


def finish(total_any, halves_ref, ids_any, rw_any, dtok_ref, dprob_ref, grad_ref, total_ref, ids_ref, rw_ref, sem):
    tok, width = dtok_ref.shape
    grad_copy = pltpu.make_async_copy(halves_ref, grad_ref, sem.at[0])
    total_copy = pltpu.make_async_copy(total_any, total_ref, sem.at[1])
    ids_copy = pltpu.make_async_copy(ids_any, ids_ref, sem.at[2])
    rw_copy = pltpu.make_async_copy(rw_any, rw_ref, sem.at[3])
    for copy in (ids_copy, rw_copy, total_copy, grad_copy):
        copy.start()
    total_copy.wait()
    dtok_ref[...] = total_ref[:, 0:width].astype(BF16)
    probs = total_ref[:, width:width + LANES].astype(BF16)
    name = lax.broadcasted_iota(jnp.int32, (LANES, LANES), 0)
    other = lax.broadcasted_iota(jnp.int32, (LANES, LANES), 1)
    same = jnp.where(name == other, 1.0, 0.0).astype(BF16)
    probs = dot_t(same, probs)
    ids_copy.wait()
    rw_copy.wait()
    name = lax.broadcasted_iota(jnp.int32, (LANES, tok), 0)
    slot = lax.broadcasted_iota(jnp.int32, (4, tok), 0)
    values = jnp.zeros((4, tok), F32)
    for k in range(4):
        value = jnp.sum(jnp.where(name == ids_ref[k:k + 1, :], probs, 0.0), axis=0, keepdims=True)
        values = jnp.where(slot == k, value, values)
    dprob_ref[...] = (values / rw_ref[...].astype(F32)).astype(BF16)
    grad_copy.wait()


def local(sizes, tokens, upstream, expert_ids, route_weight, gate_weight, up_weight, down_weight):
    nx, ny, nz = sizes
    tok, width = tokens.shape
    hid = gate_weight.shape[1]
    half_hid, hidden = hid // 2, hid * nx
    half, batches = nz // 2, nz // 4
    wide, block, quarter = width + LANES, 4 * CAP, width // 4
    count = ny * block
    vmem = pl.BlockSpec(memory_space=pltpu.VMEM)
    hbm = pl.BlockSpec(memory_space=pltpu.HBM)
    anywhere = pl.BlockSpec(memory_space=pl.ANY)
    ids, scales = expert_ids.T, route_weight.T

    def stay(value):
        return pltpu.with_memory_space_constraint(value, pltpu.HBM)

    total, halves = pl.pallas_call(
        functools.partial(kernel, sizes),
        out_shape=(
            jax.ShapeDtypeStruct((tok, wide), F32),
            jax.ShapeDtypeStruct((2, half_hid, width), F32),
        ),
        in_specs=[hbm] * 7,
        out_specs=(vmem, vmem),
        scratch_shapes=[
            pltpu.VMEM((tok, LANES), BF16),
            pltpu.VMEM((nz, tok, wide), BF16),
            pltpu.VMEM((nz, tok, width), BF16),
            pltpu.VMEM((batches, 4 * tok, count), BF16),
            pltpu.VMEM((nz // 2, ny, block, width), BF16),
            pltpu.VMEM((nz // 2, ny, block, width), BF16),
            pltpu.VMEM((3, nx, 2, half_hid, width), BF16),
            pltpu.VMEM((batches, 2 * count, hidden), BF16),
            pltpu.VMEM((count, hidden), BF16),
            pltpu.VMEM((count, hidden), BF16),
            pltpu.VMEM((batches, ny, block, wide), BF16),
            pltpu.VMEM((batches, ny, block, wide), BF16),
            pltpu.VMEM((nz, tok, wide), F32),
            pltpu.VMEM((half + 1, tok, wide), BF16),
            pltpu.VMEM((half, tok, wide), BF16),
            pltpu.VMEM((half + 1, tok, wide), BF16),
            pltpu.VMEM((half, tok, wide), BF16),
            pltpu.VMEM((nx, 2, half_hid, width), F32),
            pltpu.VMEM((nx, half_hid, width), BF16),
            pltpu.VMEM((nx, half_hid, width), BF16),
            pltpu.VMEM((nx, half_hid, width), BF16),
            pltpu.VMEM((nx, half_hid, width), BF16),
            pltpu.VMEM((half_hid, width), F32),
            pltpu.VMEM((half_hid, width), F32),
            pltpu.VMEM((4, tok), jnp.int32),
            pltpu.VMEM((4, tok), BF16),
            pltpu.VMEM((3, 2, ny, block, quarter), BF16),
            pltpu.VMEM((3, 2, ny, block, quarter), BF16),
            pltpu.VMEM((2 * count, width), BF16),
            pltpu.VMEM((4, 2 * count, 6 * count), BF16),
            pltpu.VMEM((4, count, quarter), BF16),
            pltpu.VMEM((count, LANES), BF16),
            pltpu.VMEM((2 * count, 4 * count), BF16),
            pltpu.VMEM((count, 4 * count), BF16),
            pltpu.VMEM((2, ny, block, quarter + LANES), BF16),
            pltpu.VMEM((2, ny, block // 2, quarter + LANES), BF16),
            pltpu.VMEM((2, ny, block, quarter + LANES), BF16),
            pltpu.VMEM((2, ny, block // 2, quarter + LANES), BF16),
            pltpu.VMEM((2, 4, tok, count), BF16),
            pltpu.VMEM((2, 2, tok, count // 2), BF16),
            pltpu.SemaphoreType.DMA((256,)),
            pltpu.SemaphoreType.DMA((256,)),
            pltpu.SemaphoreType.DMA((10,)),
        ],
        compiler_params=pltpu.CompilerParams(
            collective_id=0, has_side_effects=True, vmem_limit_bytes=48 << 20
        ),
    )(
        stay(tokens), stay(upstream), stay(ids), stay(scales),
        stay(gate_weight[0]), stay(up_weight[0]), stay(down_weight[0]),
    )
    d_tokens, d_probs, grad = pl.pallas_call(
        finish,
        out_shape=(
            jax.ShapeDtypeStruct((tok, width), BF16),
            jax.ShapeDtypeStruct((4, tok), BF16),
            jax.ShapeDtypeStruct((2, half_hid, width), F32),
        ),
        in_specs=[anywhere, anywhere, hbm, hbm],
        out_specs=(vmem, vmem, anywhere),
        scratch_shapes=[
            pltpu.VMEM((tok, wide), F32), pltpu.VMEM((4, tok), jnp.int32),
            pltpu.VMEM((4, tok), BF16), pltpu.SemaphoreType.DMA((4,)),
        ],
        compiler_params=pltpu.CompilerParams(vmem_limit_bytes=8 << 20),
    )(total, halves, stay(ids), stay(scales))
    return d_tokens, d_probs.T, grad.reshape(1, hid, width)


def build(mesh, ny):
    sizes = (mesh.shape["dp"], ny, mesh.shape["ep"] // ny)
    flat = P(("rep", "ep", "dp"), None)
    split = P("ep", "dp", None)
    return jax.shard_map(
        functools.partial(local, sizes),
        mesh=mesh,
        in_specs=(flat, flat, flat, flat, split, split, split),
        out_specs=(flat, flat, split),
        check_vma=False,
    )


def solution(mesh):
    return build(mesh, 4)
```
